256 devices in a mesh: gy: 32 (over x_hi, z, core), gz: 8 (over x_lo, y).
Axes of the slice: x: 4 (x_hi: 2, x_lo: 2; x = x_hi * 2 + x_lo), y: 4, z: 8, core: 2. Of those that a mesh axis runs over, the one named last changes fastest.
Arguments:
- populations: float32 [19, 4, 256, 8192], P(None, None, 'gy', 'gz'), may hold values from 0 to 1, as said below
- solid_mask: int32 [4, 256, 8192], P(None, 'gy', 'gz'), may hold values 0 or 1
- body_force: float32 [3], replicated, may hold values from 0.002 to 0.008
Outputs:
- density: float32 [4, 256, 8192], P(None, 'gy', 'gz')
- velocity: float32 [3, 4, 256, 8192], P(None, None, 'gy', 'gz')
The draws below stay inside these ranges and needn't reach their ends.
Inputs may be any that keep to these rules, and one draw needn't show every extreme that they name: `populations`: every population is positive, near its lattice weight times one.
All inputs are finite; a program needn't handle non-finite values. No bound on the sum of `solid_mask` on one device may be relied on, other than what follows from the above.
Results may differ from the reference program's by a relative error of at most 0.0003.
Values sent between devices are 32-bit elements; how exact they have to be, the bound alone decides.
No kernel may reach another device: no remote copies, remote signals or barrier semaphores. Data moves between devices by JAX's collectives and lax.ppermute only.
A program may use at most 64 MiB of HBM per device.

```python
import jax
import jax.numpy as jnp
from jax import lax

PLANES = 4
STEPS = 3
NY = 256
NZ = 8192


def draw_populations(key, part):
    weight_list = [1.0 / 3.0] + [1.0 / 18.0] * 6 + [1.0 / 36.0] * 12
    lift_list = [0, 0, 0, 0, 0, 1, -1, 0, 0, 0, 0, 1, -1, -1, 1, 1, -1, -1, 1]
    wfull = jnp.asarray(weight_list, dtype=jnp.float32).reshape(19, 1, 1, 1)
    lift = jnp.asarray(lift_list, dtype=jnp.float32).reshape(19, 1, 1, 1)
    shape = (19, PLANES, NY, NZ)
    rough = 1.0 + jax.random.uniform(key, shape, jnp.float32, -0.4, 0.4)
    return wfull * rough * (1.0 + 0.09 * lift)


def with_ends(values, key, least, top_value):
    longest = values.shape.index(max(values.shape))
    spots = []
    for shift in (0, 1):
        where = [jax.random.randint(jax.random.fold_in(key, axis), (), 0, length) for axis, length in enumerate(values.shape)]
        where[longest] = (where[longest] + shift) % values.shape[longest]
        spots.append(tuple(where))
    return values.at[spots[0]].set(least).at[spots[1]].set(top_value)


def setup_inputs(seed: int = 0) -> dict:
    streams_of = jax.random.split(jax.random.key(seed), 4)
    return {
        "populations": draw_populations(jax.random.fold_in(streams_of[3], 71), 0),
        "solid_mask": with_ends((jax.random.randint(streams_of[1], (PLANES, NY, NZ), 0, 4) < 1).astype(jnp.int32), jax.random.fold_in(streams_of[1], 1), 0, 1),
        "body_force": jnp.clip(jax.random.uniform(streams_of[2], (3,), jnp.float32, 0.002, 0.008), 0.002, 0.008),
    }


velocities = [(0, 0, 0), (1, 0, 0), (-1, 0, 0), (0, 1, 0), (0, -1, 0), (0, 0, 1), (0, 0, -1),
              (1, 1, 0), (-1, -1, 0), (1, -1, 0), (-1, 1, 0), (1, 0, 1), (-1, 0, -1),
              (1, 0, -1), (-1, 0, 1), (0, 1, 1), (0, -1, -1), (0, 1, -1), (0, -1, 1)]
opposite = [0, 2, 1, 4, 3, 6, 5, 8, 7, 10, 9, 12, 11, 14, 13, 16, 15, 18, 17]
lattice_weights = [1.0 / 3.0] + [1.0 / 18.0] * 6 + [1.0 / 36.0] * 12
reference_mach = 0.05


def invert_list(matrix):
    count = len(matrix)
    work = [list(matrix[i]) + [1.0 if i == j else 0.0 for j in range(count)] for i in range(count)]
    for column in range(count):
        pivot = column
        for row in range(column + 1, count):
            if abs(work[row][column]) > abs(work[pivot][column]):
                pivot = row
        work[column], work[pivot] = work[pivot], work[column]
        factor = work[column][column]
        work[column] = [entry / factor for entry in work[column]]
        for row in range(count):
            if row != column:
                scale = work[row][column]
                if scale != 0.0:
                    work[row] = [a - scale * b for a, b in zip(work[row], work[column])]
    return [line[count:] for line in work]


def relax_table():
    columns = []
    for shift_x, shift_y, shift_z in velocities:
        columns.append([1, shift_x, shift_y, shift_z, shift_x ** 2, shift_y ** 2, shift_z ** 2,
                        shift_x * shift_y, shift_x * shift_z, shift_y * shift_z,
                        shift_x ** 2 * shift_y, shift_x ** 2 * shift_z, shift_y ** 2 * shift_x,
                        shift_y ** 2 * shift_z, shift_z ** 2 * shift_x, shift_z ** 2 * shift_y,
                        shift_x ** 2 * shift_y ** 2, shift_x ** 2 * shift_z ** 2, shift_y ** 2 * shift_z ** 2])
    moments = [[float(columns[k][a]) for k in range(19)] for a in range(19)]
    inverse = invert_list(moments)
    rates = [0.0] * 4 + [1.25] * 6 + [1.6] * 6 + [1.3] * 3
    table = [[sum(inverse[i][a] * rates[a] * moments[a][j] for a in range(19)) for j in range(19)]
             for i in range(19)]
    return jnp.asarray(table, dtype=jnp.float32)


def collide(current, body_force, relax):
    cvec = jnp.asarray(velocities, dtype=jnp.float32)
    wvec = jnp.asarray(lattice_weights, dtype=jnp.float32)
    wfull = wvec.reshape(19, 1, 1, 1)
    density = jnp.sum(current, axis=0)
    momentum = jnp.tensordot(cvec.T, current, axes=1, precision=lax.Precision.HIGHEST)
    flow = momentum / density
    projected = jnp.tensordot(cvec, flow, axes=1, precision=lax.Precision.HIGHEST)
    speed_sq = jnp.sum(flow * flow, axis=0)
    equilibrium = wfull * density * (1.0 + 3.0 * projected + 4.5 * projected * projected - 1.5 * speed_sq)
    departure = (current - equilibrium).reshape(19, -1)
    change = jnp.dot(relax, departure, precision=lax.Precision.HIGHEST).reshape(current.shape)
    forcing = 3.0 * wvec * jnp.dot(cvec, body_force, precision=lax.Precision.HIGHEST)
    return current - change + forcing.reshape(19, 1, 1, 1)


def stream(padded, solid_pad, center):
    planes, across, length = center.shape[1:]
    result = []
    for k in range(19):
        shift_x, shift_y, shift_z = velocities[k]
        source = padded[k, 1 - shift_x:1 - shift_x + planes, 1 - shift_y:1 - shift_y + across,
                        1 - shift_z:1 - shift_z + length]
        blocked = solid_pad[1 - shift_x:1 - shift_x + planes, 1 - shift_y:1 - shift_y + across,
                            1 - shift_z:1 - shift_z + length]
        result.append(jnp.where(blocked > 0, center[opposite[k]], source))
    return jnp.stack(result)


def moments_out(current, solid_core):
    cvec = jnp.asarray(velocities, dtype=jnp.float32)
    fluid = (1 - solid_core).astype(jnp.float32)
    density = jnp.sum(current, axis=0)
    momentum = jnp.tensordot(cvec.T, current, axes=1, precision=lax.Precision.HIGHEST)
    return density * fluid, momentum / density / reference_mach * fluid


def reference(populations, solid_mask, body_force):
    relax = relax_table()
    solid_pad = jnp.pad(solid_mask, ((0, 0), (1, 1), (1, 1)), mode="wrap")
    solid_pad = jnp.pad(solid_pad, ((1, 1), (0, 0), (0, 0)), constant_values=1)
    current = populations
    for sweep in range(STEPS):
        relaxed = collide(current, body_force, relax)
        padded = jnp.pad(relaxed, ((0, 0), (0, 0), (1, 1), (1, 1)), mode="wrap")
        padded = jnp.pad(padded, ((0, 0), (1, 1), (0, 0), (0, 0)))
        current = stream(padded, solid_pad, relaxed)
    return moments_out(current, solid_mask)
```

```python
import jax
import jax.numpy as jnp
from jax import lax
from jax.experimental import pallas as pl
from jax.experimental.pallas import tpu as pltpu
from jax.sharding import PartitionSpec as P

VEL = [
    (0, 0, 0),
    (1, 0, 0),
    (-1, 0, 0),
    (0, 1, 0),
    (0, -1, 0),
    (0, 0, 1),
    (0, 0, -1),
    (1, 1, 0),
    (-1, -1, 0),
    (1, -1, 0),
    (-1, 1, 0),
    (1, 0, 1),
    (-1, 0, -1),
    (1, 0, -1),
    (-1, 0, 1),
    (0, 1, 1),
    (0, -1, -1),
    (0, 1, -1),
    (0, -1, 1),
]
OPP = [VEL.index((-x, -y, -z)) for x, y, z in VEL]
FLIP = [VEL.index((x, -y, z)) for x, y, z in VEL]
IN = [k for k in range(19) if VEL[k][1] == 1]
OUT = [FLIP[k] for k in IN]
FLAT = [k for k in range(19) if VEL[k][1] == 0]
LOCAL = FLAT + OUT
NMSG = 24
MACH = 0.05
BIG = 1e30
NAN = float("nan")
F32 = jnp.float32


def lanes():
    return lax.broadcasted_iota(jnp.int32, (8, 128), 1)


def rows():
    return lax.broadcasted_iota(jnp.int32, (8, 128), 0)


def collide(f, force):
    fx, fy, fz = force
    sx, dx = f[1] + f[2], f[1] - f[2]
    sy, dy = f[3] + f[4], f[3] - f[4]
    sz, dz = f[5] + f[6], f[5] - f[6]

    def plane(a):
        big, small = f[a] + f[a + 1], f[a] - f[a + 1]
        big2, small2 = f[a + 2] + f[a + 3], f[a + 2] - f[a + 3]
        return big + big2, big - big2, small + small2, small - small2

    nxy, mxy, tyyx, txxy = plane(7)
    nxz, mxz, tzzx, txxz = plane(11)
    nyz, myz, tzzy, tyyz = plane(15)
    jx = dx + (tyyx + tzzx)
    jy = dy + (txxy + tzzy)
    jz = dz + (txxz + tyyz)
    mxx = sx + (nxy + nxz)
    myy = sy + (nxy + nyz)
    mzz = sz + (nxz + nyz)
    rho = ((f[0] + mxx) + (sy + sz)) + nyz
    inv = 0.3125 / rho
    vx, vy, vz = jx * inv, jy * inv, jz * inv
    gx, gy, gz = jx * vx, jy * vy, jz * vz
    third = rho * (1.25 / 6.0)
    hx = (third + (gx + gx)) - 0.125 * mxx
    hy = (third + (gy + gy)) - 0.125 * myy
    hz = (third + (gz + gz)) - 0.125 * mzz
    mxy = jx * vy - 0.0625 * mxy
    mxz = jx * vz - 0.0625 * mxz
    myz = jy * vz - 0.0625 * myz
    base = rho * (1.3 / 36.0) + (gx + gy + gz) * (1.3 / 12.0 / 0.3125)
    nxy = (base - 0.52 * gz) - 0.075 * nxy
    nxz = (base - 0.52 * gy) - 0.075 * nxz
    nyz = (base - 0.52 * gx) - 0.075 * nyz
    bx = jx * (0.4 / 3.0) + fx * (1.0 / 12.0)
    by = jy * (0.4 / 3.0) + fy * (1.0 / 12.0)
    bz = jz * (0.4 / 3.0) + fz * (1.0 / 12.0)
    tyyx, tzzx = bx - 0.15 * tyyx, bx - 0.15 * tzzx
    txxy, tzzy = by - 0.15 * txxy, by - 0.15 * tzzy
    txxz, tyyz = bz - 0.15 * txxz, bz - 0.15 * tyyz
    out = [None] * 19

    def axis(a, half, j, force_a, n1, n2, t1, t2):
        even = half - 2.0 * (n1 + n2)
        odd = 0.5 * (j + force_a) - 2.0 * (t1 + t2)
        out[a], out[a + 1] = even + odd, even - odd

    def edge(a, n, m, t1, t2):
        big, big2 = n + m, n - m
        small, small2 = t1 + t2, t1 - t2
        out[a], out[a + 1] = big + small, big - small
        out[a + 2], out[a + 3] = big2 + small2, big2 - small2

    axis(1, hx, jx, fx, nxy, nxz, tyyx, tzzx)
    axis(3, hy, jy, fy, nxy, nyz, txxy, tzzy)
    axis(5, hz, jz, fz, nxz, nyz, txxz, tyyz)
    edge(7, nxy, mxy, tyyx, txxy)
    edge(11, nxz, mxz, tzzx, txxz)
    edge(15, nyz, myz, tzzy, tyyz)
    out[0] = rho - 2.0 * (hx + hy + hz) + 4.0 * (nxy + nxz + nyz)
    return out


def along_z(get, t, cz, lane):
    cur = get(t)
    if cz == 0:
        return cur
    if cz == 1:
        before = get(jnp.where(t == 0, 8, t - 1))
        return pltpu.roll(jnp.where(lane == 127, before, cur), 1, axis=1)
    after = get(jnp.where(t == 8, 0, t + 1))
    return pltpu.roll(jnp.where(lane == 0, after, cur), 127, axis=1)


def stream_own(ref, halo, p, t, lane, row):
    f = []
    for k in range(19):
        cx, cy, cz = VEL[k]
        own = ref[OPP[k], t, 8 * p : 8 * p + 8, :]
        q = p - cx
        if k == 0 or q < 0 or q > 3:
            f.append(own)
            continue

        def get(s, k=k, q=q, cy=cy):
            v = ref[k, s, 8 * q : 8 * q + 8, :]
            if cy == 0 or halo is None:
                return v
            if cy == 1:
                at, i, sub = 7, IN.index(k), q
            else:
                at, i, sub = 0, IN.index(FLIP[k]), 4 + q
            rim = jnp.broadcast_to(halo[i, s, sub : sub + 1, :], (8, 128))
            return jnp.where(row == at, rim, v)

        v = along_z(get, t, cz, lane)
        if cy == 1:
            v = pltpu.roll(v, 1, axis=0)
        elif cy == -1:
            v = pltpu.roll(v, 7, axis=0)
        f.append(jnp.where(v < BIG, v, own))
    return f


def stream_rim(get, own, k, t, lane, row):
    cx, _, cz = VEL[k]
    v = along_z(get, t, cz, lane)
    if cx:
        v = pltpu.roll(v, cx % 8, axis=0)
        wall = (row & 3) == (0 if cx == 1 else 3)
        v = jnp.where(wall, NAN, v)
    return jnp.where(v < BIG, v, own)


def edges(ref, k, t, lower, upper):
    a = ref[k, t, pl.ds(lower, 4, stride=8), :]
    b = ref[FLIP[k], t, pl.ds(upper, 4, stride=8), :]
    return jnp.concatenate([a, b], axis=0)


def force_of(force_ref):
    return force_ref[0], force_ref[1], force_ref[2]


def rim_force(force, row):
    fx, fy, fz = force
    return fx, jnp.where(row < 4, fy, -fy), fz


def pack_kernel(first, last, mask_first, mask_last, out0, out1):
    lane = lanes()
    even = lax.rem(lax.axis_index("gz"), 2) == 0
    group = lane // 4
    for tile in range(3):
        left = jnp.zeros((8, 128), F32)
        right = jnp.zeros((8, 128), F32)
        for s in range(32):
            i = tile * 32 + s
            if i >= 76:
                break
            k, p = i // 4, i % 4
            a, b = first[k, p], last[k, p]
            if k == 0:
                a = jnp.where(mask_first[p] > 0, NAN, a)
                b = jnp.where(mask_last[p] > 0, NAN, b)
            if s:
                a = pltpu.roll(a, 4 * s, axis=1)
            if s != 31:
                b = pltpu.roll(b, 4 * s + 4, axis=1)
            left = jnp.where(group == s, a, left)
            right = jnp.where(group == s, b, right)
        out0[tile] = jnp.where(even, right, left)
        out1[tile] = jnp.where(even, left, right)


def first_kernel(force_ref, pop, mask, got0, got1, r2, edge, near, far, r1, f1, rim):
    lane, row = lanes(), rows()
    force = force_of(force_ref)
    even_z = lax.rem(lax.axis_index("gz"), 2) == 0
    even_y = lax.rem(lax.axis_index("gy"), 2) == 0
    for tile in range(3):
        a, b = got0[tile], got1[tile]
        from_right = jnp.where(even_z, a, b)
        from_left = jnp.where(even_z, b, a)
        for s in range(32):
            i = tile * 32 + s
            if i >= 76:
                break
            k, p = i // 4, i % 4
            x = pltpu.roll(from_right, 128 - 4 * s, axis=1) if s else from_right
            y = pltpu.roll(from_left, 124 - 4 * s, axis=1) if s != 31 else from_left
            rim[k, p] = jnp.where(lane < 64, x, y)

    def put(t, p, f):
        g = collide(f, force)
        for k in range(19):
            r1[k, t, 8 * p : 8 * p + 8, :] = g[k]

    @pl.loop(0, 8)
    def _(t):
        at = pl.ds(pl.multiple_of(t * 128, 128), 128)
        for p in range(4):
            f = [pop[k, p, :, at] for k in range(19)]
            f[0] = jnp.where(mask[p, :, at] > 0, NAN, f[0])
            put(t, p, f)

    for p in range(4):
        put(8, p, [rim[k, p] for k in range(19)])

    @pl.loop(0, 9)
    def _(t):
        for p in range(4):
            f = stream_own(r1, None, p, t, lane, row)
            for k in range(19):
                f1[k, t, 8 * p : 8 * p + 8, :] = f[k]
            g = collide(f, force)
            for k in range(19):
                r2[k, t, 8 * p : 8 * p + 8, :] = g[k]

    @pl.loop(0, 9)
    def _(t):
        values = [edges(r1, k, t, 0, 7) for k in OUT]
        values += [edges(f1, k, t, 0, 7) for k in LOCAL]
        values += [edges(r2, k, t, 1, 6) for k in OUT]
        for i, v in enumerate(values):
            edge[i, t] = v
            w = jnp.where(even_y, pltpu.roll(v, 4, axis=0), v)
            near[i, t] = w[0:4]
            far[i, t] = w[4:8]


def last_kernel(
    force_ref, r2_hbm, edge, near, far, mask, density, velocity, r2, r3, got, r2h, r2e, r3h, sem
):
    copy = pltpu.make_async_copy(r2_hbm, r2, sem)
    copy.start()
    lane, row = lanes(), rows()
    force = force_of(force_ref)
    force_rim = rim_force(force, row)
    even_y = lax.rem(lax.axis_index("gy"), 2) == 0

    @pl.loop(0, 9)
    def _(t):
        for i in range(NMSG):
            v = jnp.concatenate([near[i, t], far[i, t]], axis=0)
            got[i, t] = jnp.where(even_y, pltpu.roll(v, 4, axis=0), v)

    copy.wait()

    @pl.loop(0, 9)
    def _(t):
        f = [None] * 19
        for i, k in enumerate(LOCAL):
            f[k] = edge[5 + i, t]
        for i, k in enumerate(IN):
            own = edge[OUT.index(OPP[k]), t]
            f[k] = stream_rim(lambda s, i=i: got[i, s], own, k, t, lane, row)
        g = collide(f, force_rim)
        for k in range(19):
            r2[k, t, pl.ds(0, 4, stride=8), :] = g[k][0:4]
            r2[FLIP[k], t, pl.ds(7, 4, stride=8), :] = g[k][4:8]
        for i, k in enumerate(OUT):
            r2e[i, t] = g[k]
        f = [None] * 19
        for i, k in enumerate(LOCAL):
            f[FLIP[k]] = got[5 + i, t]
        for i, k in enumerate(OUT):
            own = got[IN.index(OPP[k]), t]
            f[k] = stream_rim(lambda s, i=i: edge[i, s], own, k, t, lane, row)
        g = collide(f, force_rim)
        for i, k in enumerate(IN + FLAT + OUT):
            r2h[i, t] = g[k]

    place = {k: i for i, k in enumerate(IN + FLAT + OUT)}

    @pl.loop(0, 9)
    def _(t):
        f = [None] * 19
        for k in range(19):
            own = r2h[place[OPP[k]], t]
            if k == 0:
                f[k] = own
            elif k in FLAT:
                f[k] = stream_rim(lambda s, k=k: r2h[place[k], s], own, k, t, lane, row)
            elif k in IN:
                f[k] = stream_rim(lambda s, k=k: got[19 + IN.index(k), s], own, k, t, lane, row)
            else:
                f[k] = stream_rim(lambda s, k=k: r2e[OUT.index(k), s], own, k, t, lane, row)
        g = collide(f, force_rim)
        for i, k in enumerate(IN):
            r3h[i, t] = g[k]
        for p in range(4):
            g = collide(stream_own(r2, r2h, p, t, lane, row), force)
            for k in range(19):
                r3[k, t, 8 * p : 8 * p + 8, :] = g[k]

    @pl.loop(0, 8)
    def _(t):
        at = pl.ds(pl.multiple_of(t * 128, 128), 128)
        for p in range(4):
            f = stream_own(r3, r3h, p, t, lane, row)
            rho = f[0]
            for k in range(1, 19):
                rho = rho + f[k]
            solid = mask[p, :, at] > 0
            density[p, :, at] = jnp.where(solid, 0.0, rho)
            inv = (1.0 / MACH) / rho
            for a in range(3):
                plus = [f[k] for k in range(19) if VEL[k][a] == 1]
                minus = [f[k] for k in range(19) if VEL[k][a] == -1]
                j = plus[0] - minus[0]
                for x, y in zip(plus[1:], minus[1:]):
                    j = j + (x - y)
                velocity[a, p, :, at] = jnp.where(solid, 0.0, j * inv)


VMEM = pl.BlockSpec(memory_space=pltpu.VMEM)
SMEM = pl.BlockSpec(memory_space=pltpu.SMEM)
ANY = pl.BlockSpec(memory_space=pl.ANY)


def params():
    return pltpu.CompilerParams(vmem_limit_bytes=48 * 1024 * 1024)


def sds(*shape):
    return jax.ShapeDtypeStruct(shape, F32)


def swap(x, axis, parity):
    count = lax.axis_size(axis)
    pairs = [(i, (i + 1) % count if i % 2 == parity else (i - 1) % count) for i in range(count)]
    return lax.ppermute(x, axis, pairs)


def local(pop, mask, force):
    z0, z1 = pl.pallas_call(
        pack_kernel,
        out_shape=(sds(3, 8, 128), sds(3, 8, 128)),
        grid=(1,),
        in_specs=[
            pl.BlockSpec((19, 4, 8, 128), lambda i: (0, 0, 0, 0)),
            pl.BlockSpec((19, 4, 8, 128), lambda i: (0, 0, 0, 7)),
            pl.BlockSpec((4, 8, 128), lambda i: (0, 0, 0)),
            pl.BlockSpec((4, 8, 128), lambda i: (0, 0, 7)),
        ],
        out_specs=(
            pl.BlockSpec((3, 8, 128), lambda i: (0, 0, 0)),
            pl.BlockSpec((3, 8, 128), lambda i: (0, 0, 0)),
        ),
        compiler_params=params(),
        name="pack",
    )(pop, pop, mask, mask)
    got0 = swap(z0, "gz", 0)
    got1 = swap(z1, "gz", 1)
    r2, edge, near, far = pl.pallas_call(
        first_kernel,
        out_shape=(sds(19, 9, 32, 128), sds(NMSG, 9, 8, 128), sds(NMSG, 9, 4, 128), sds(NMSG, 9, 4, 128)),
        in_specs=[SMEM, VMEM, VMEM, VMEM, VMEM],
        out_specs=(VMEM, VMEM, VMEM, VMEM),
        scratch_shapes=[
            pltpu.VMEM((19, 9, 32, 128), F32),
            pltpu.VMEM((19, 9, 32, 128), F32),
            pltpu.VMEM((19, 4, 8, 128), F32),
        ],
        compiler_params=params(),
        name="first",
    )(force, pop, mask, got0, got1)
    far = swap(far, "gy", 1)
    near = swap(near, "gy", 0)
    return pl.pallas_call(
        last_kernel,
        out_shape=(sds(4, 8, 1024), sds(3, 4, 8, 1024)),
        in_specs=[SMEM, ANY, VMEM, VMEM, VMEM, VMEM],
        out_specs=(VMEM, VMEM),
        scratch_shapes=[
            pltpu.VMEM((19, 9, 32, 128), F32),
            pltpu.VMEM((19, 9, 32, 128), F32),
            pltpu.VMEM((NMSG, 9, 8, 128), F32),
            pltpu.VMEM((19, 9, 8, 128), F32),
            pltpu.VMEM((5, 9, 8, 128), F32),
            pltpu.VMEM((5, 9, 8, 128), F32),
            pltpu.SemaphoreType.DMA,
        ],
        compiler_params=params(),
        name="last",
    )(force, r2, edge, near, far, mask)


def solution(mesh):
    return jax.shard_map(
        local,
        mesh=mesh,
        in_specs=(P(None, None, "gy", "gz"), P(None, "gy", "gz"), P()),
        out_specs=(P(None, "gy", "gz"), P(None, None, "gy", "gz")),
        check_vma=False,
    )
```

```python
import jax
import jax.numpy as jnp
from jax import lax
from jax.experimental import pallas as pl
from jax.experimental.pallas import tpu as pltpu
from jax.sharding import PartitionSpec as P

VEL = [
    (0, 0, 0),
    (1, 0, 0),
    (-1, 0, 0),
    (0, 1, 0),
    (0, -1, 0),
    (0, 0, 1),
    (0, 0, -1),
    (1, 1, 0),
    (-1, -1, 0),
    (1, -1, 0),
    (-1, 1, 0),
    (1, 0, 1),
    (-1, 0, -1),
    (1, 0, -1),
    (-1, 0, 1),
    (0, 1, 1),
    (0, -1, -1),
    (0, 1, -1),
    (0, -1, 1),
]
OPP = [VEL.index((-x, -y, -z)) for x, y, z in VEL]
FLIP = [VEL.index((x, -y, z)) for x, y, z in VEL]
IN = [k for k in range(19) if VEL[k][1] == 1]
OUT = [FLIP[k] for k in IN]
FLAT = [k for k in range(19) if VEL[k][1] == 0]
LOCAL = FLAT + OUT
NMSG = 24
MACH = 0.05
BIG = 1e30
NAN = float("nan")
F32 = jnp.float32


def lanes():
    return lax.broadcasted_iota(jnp.int32, (8, 128), 1)


def rows():
    return lax.broadcasted_iota(jnp.int32, (8, 128), 0)


def collide(f, force):
    fx, fy, fz = force
    sx, dx = f[1] + f[2], f[1] - f[2]
    sy, dy = f[3] + f[4], f[3] - f[4]
    sz, dz = f[5] + f[6], f[5] - f[6]

    def plane(a):
        big, small = f[a] + f[a + 1], f[a] - f[a + 1]
        big2, small2 = f[a + 2] + f[a + 3], f[a + 2] - f[a + 3]
        return big + big2, big - big2, small + small2, small - small2

    nxy, mxy, tyyx, txxy = plane(7)
    nxz, mxz, tzzx, txxz = plane(11)
    nyz, myz, tzzy, tyyz = plane(15)
    jx = dx + (tyyx + tzzx)
    jy = dy + (txxy + tzzy)
    jz = dz + (txxz + tyyz)
    mxx = sx + (nxy + nxz)
    myy = sy + (nxy + nyz)
    mzz = sz + (nxz + nyz)
    rho = ((f[0] + mxx) + (sy + sz)) + nyz
    inv = 0.3125 / rho
    vx, vy, vz = jx * inv, jy * inv, jz * inv
    gx, gy, gz = jx * vx, jy * vy, jz * vz
    third = rho * (1.25 / 6.0)
    hx = (third + (gx + gx)) - 0.125 * mxx
    hy = (third + (gy + gy)) - 0.125 * myy
    hz = (third + (gz + gz)) - 0.125 * mzz
    mxy = jx * vy - 0.0625 * mxy
    mxz = jx * vz - 0.0625 * mxz
    myz = jy * vz - 0.0625 * myz
    base = rho * (1.3 / 36.0) + (gx + gy + gz) * (1.3 / 12.0 / 0.3125)
    nxy = (base - 0.52 * gz) - 0.075 * nxy
    nxz = (base - 0.52 * gy) - 0.075 * nxz
    nyz = (base - 0.52 * gx) - 0.075 * nyz
    bx = jx * (0.4 / 3.0) + fx * (1.0 / 12.0)
    by = jy * (0.4 / 3.0) + fy * (1.0 / 12.0)
    bz = jz * (0.4 / 3.0) + fz * (1.0 / 12.0)
    tyyx, tzzx = bx - 0.15 * tyyx, bx - 0.15 * tzzx
    txxy, tzzy = by - 0.15 * txxy, by - 0.15 * tzzy
    txxz, tyyz = bz - 0.15 * txxz, bz - 0.15 * tyyz
    out = [None] * 19

    def axis(a, half, j, force_a, n1, n2, t1, t2):
        even = half - 2.0 * (n1 + n2)
        odd = 0.5 * (j + force_a) - 2.0 * (t1 + t2)
        out[a], out[a + 1] = even + odd, even - odd

    def edge(a, n, m, t1, t2):
        big, big2 = n + m, n - m
        small, small2 = t1 + t2, t1 - t2
        out[a], out[a + 1] = big + small, big - small
        out[a + 2], out[a + 3] = big2 + small2, big2 - small2

    axis(1, hx, jx, fx, nxy, nxz, tyyx, tzzx)
    axis(3, hy, jy, fy, nxy, nyz, txxy, tzzy)
    axis(5, hz, jz, fz, nxz, nyz, txxz, tyyz)
    edge(7, nxy, mxy, tyyx, txxy)
    edge(11, nxz, mxz, tzzx, txxz)
    edge(15, nyz, myz, tzzy, tyyz)
    out[0] = rho - 2.0 * (hx + hy + hz) + 4.0 * (nxy + nxz + nyz)
    return out


def along_z(get, t, cz, lane, split=False):
    def at(s):
        return get(None if split and s == 8 else s)

    if isinstance(t, int):
        prev, succ = (t + 8) % 9, (t + 1) % 9
    elif split:
        prev, succ = t - 1, t + 1
    else:
        prev, succ = jnp.where(t == 0, 8, t - 1), jnp.where(t == 8, 0, t + 1)
    cur = at(t) if isinstance(t, int) else get(t)
    if cz == 0:
        return cur
    if cz == 1:
        before = at(prev) if isinstance(t, int) else get(prev)
        return pltpu.roll(jnp.where(lane == 127, before, cur), 1, axis=1)
    after = at(succ) if isinstance(t, int) else get(succ)
    return pltpu.roll(jnp.where(lane == 0, after, cur), 127, axis=1)


def stream_own(load, halo, p, t, lane, row):
    split = halo is None
    f = []
    for k in range(19):
        cx, cy, cz = VEL[k]
        own = load(OPP[k], None if split and isinstance(t, int) and t == 8 else t, p)
        q = p - cx
        if k == 0 or q < 0 or q > 3:
            f.append(own)
            continue

        def get(s, k=k, q=q, cy=cy):
            v = load(k, s, q)
            if cy == 0 or halo is None:
                return v
            if cy == 1:
                at, i, sub = 7, IN.index(k), q
            else:
                at, i, sub = 0, IN.index(FLIP[k]), 4 + q
            rim = jnp.broadcast_to(halo[i, s, sub : sub + 1, :], (8, 128))
            return jnp.where(row == at, rim, v)

        v = along_z(get, t, cz, lane, split)
        if cy == 1:
            v = pltpu.roll(v, 1, axis=0)
        elif cy == -1:
            v = pltpu.roll(v, 7, axis=0)
        f.append(jnp.where(v < BIG, v, own))
    return f


def stream_rim(get, own, k, t, lane, row):
    cx, _, cz = VEL[k]
    v = along_z(get, t, cz, lane)
    if cx:
        v = pltpu.roll(v, cx % 8, axis=0)
        wall = (row & 3) == (0 if cx == 1 else 3)
        v = jnp.where(wall, NAN, v)
    return jnp.where(v < BIG, v, own)


def edges(ref, flipped, lower, upper):
    a = ref[pl.ds(lower, 4, stride=8), :]
    b = flipped[pl.ds(upper, 4, stride=8), :]
    return jnp.concatenate([a, b], axis=0)


def force_of(force_ref):
    return force_ref[0], force_ref[1], force_ref[2]


def rim_force(force, row):
    fx, fy, fz = force
    return fx, jnp.where(row < 4, fy, -fy), fz


GROUPS = ((0, 5), (5, 10), (10, 15), (15, 19))


def pack_kernel(pop_hbm, mask_hbm, out1, out0, first, last, mask_first, mask_last, sem):
    copies = [
        pltpu.make_async_copy(mask_hbm.at[:, :, 0:128], mask_first, sem.at[0]),
        pltpu.make_async_copy(mask_hbm.at[:, :, 896:1024], mask_last, sem.at[1]),
    ]
    for i, (a, b) in enumerate(GROUPS):
        for j, (at, to) in enumerate(((0, first), (896, last))):
            copies.append(
                pltpu.make_async_copy(
                    pop_hbm.at[a:b, :, :, at : at + 128], to.at[a:b], sem.at[2 + 2 * i + j]
                )
            )
    for copy in copies:
        copy.start()
    for copy in copies:
        copy.wait()
    lane = lanes()
    even = lax.rem(lax.axis_index("gz"), 2) == 0
    group = lane // 4
    for tile in range(3):
        left = jnp.zeros((8, 128), F32)
        right = jnp.zeros((8, 128), F32)
        for s in range(32):
            i = tile * 32 + s
            if i >= 76:
                break
            k, p = i // 4, i % 4
            a, b = first[k, p], last[k, p]
            if k == 0:
                a = jnp.where(mask_first[p] > 0, NAN, a)
                b = jnp.where(mask_last[p] > 0, NAN, b)
            if s:
                a = pltpu.roll(a, 4 * s, axis=1)
            if s != 31:
                b = pltpu.roll(b, 4 * s + 4, axis=1)
            left = jnp.where(group == s, a, left)
            right = jnp.where(group == s, b, right)
        out0[tile] = jnp.where(even, right, left)
        out1[tile] = jnp.where(even, left, right)


def rim_values(e1, e2, e3, t, force_rim, lane, row):
    own = [e1(k, t) for k in range(19)]
    values = [own[k] for k in OUT]
    for k in LOCAL:
        if k == 0:
            values.append(own[0])
        else:
            src = e1 if k in FLAT else e2
            values.append(stream_rim(lambda s, k=k, src=src: src(k, s), own[OPP[k]], k, t, lane, row))
    own = [e2(k, t) for k in range(19)]
    f = [own[0]]
    for k in range(1, 19):
        src = e2 if k in FLAT else (e1 if k in IN else e3)
        f.append(stream_rim(lambda s, k=k, src=src: src(k, s), own[OPP[k]], k, t, lane, row))
    g = collide(f, force_rim)
    return values + [g[k] for k in OUT]


def collide_kernel(force_ref, pop, mask, r1, e1, e2, e3, inner):
    lane, row = lanes(), rows()
    force = force_of(force_ref)
    force_rim = rim_force(force, row)

    @pl.loop(0, 8)
    def _(t):
        at = pl.ds(pl.multiple_of(t * 128, 128), 128)
        for p in range(4):
            f = [pop[k, p, :, at] for k in range(19)]
            f[0] = jnp.where(mask[p, :, at] > 0, NAN, f[0])
            g = collide(f, force)
            for k in range(19):
                r1[k, t, 8 * p : 8 * p + 8, :] = g[k]
        for k in range(19):
            e1[t, k] = edges(r1.at[k, t], r1.at[FLIP[k], t], 0, 7)
            e2[t, k] = edges(r1.at[k, t], r1.at[FLIP[k], t], 1, 6)
        for i, k in enumerate(OUT):
            e3[t, i] = edges(r1.at[k, t], r1.at[FLIP[k], t], 2, 5)

    @pl.loop(1, 7)
    def _(t):
        values = rim_values(
            lambda k, s: e1[s, k], lambda k, s: e2[s, k], lambda k, s: e3[s, OUT.index(k)],
            t, force_rim, lane, row,
        )
        for i, v in enumerate(values):
            inner[t - 1, i] = v


def rim_kernel(force_ref, e1, e2, e3, inner, got1, got0, r1h, edge, far, near, strip, h1, h2, h3):
    lane, row = lanes(), rows()
    force = force_of(force_ref)
    force_rim = rim_force(force, row)
    even_z = lax.rem(lax.axis_index("gz"), 2) == 0
    even_y = lax.rem(lax.axis_index("gy"), 2) == 0
    for tile in range(3):
        a, b = got0[tile], got1[tile]
        from_right = jnp.where(even_z, a, b)
        from_left = jnp.where(even_z, b, a)
        for s in range(32):
            i = tile * 32 + s
            if i >= 76:
                break
            k, p = i // 4, i % 4
            x = pltpu.roll(from_right, 128 - 4 * s, axis=1) if s else from_right
            y = pltpu.roll(from_left, 124 - 4 * s, axis=1) if s != 31 else from_left
            strip[k, p] = jnp.where(lane < 64, x, y)
    for p in range(4):
        g = collide([strip[k, p] for k in range(19)], force)
        for k in range(19):
            r1h[k, 8 * p : 8 * p + 8, :] = g[k]
    for k in range(19):
        h1[k] = edges(r1h.at[k], r1h.at[FLIP[k]], 0, 7)
        h2[k] = edges(r1h.at[k], r1h.at[FLIP[k]], 1, 6)
    for i, k in enumerate(OUT):
        h3[i] = edges(r1h.at[k], r1h.at[FLIP[k]], 2, 5)

    def put(t, i, v):
        edge[i, t] = v
        w = jnp.where(even_y, pltpu.roll(v, 4, axis=0), v)
        near[i, t] = w[0:4]
        far[i, t] = w[4:8]

    for t in (0, 7, 8):
        values = rim_values(
            lambda k, s: h1[k] if s == 8 else e1[s, k],
            lambda k, s: h2[k] if s == 8 else e2[s, k],
            lambda k, s: h3[OUT.index(k)] if s == 8 else e3[s, OUT.index(k)],
            t, force_rim, lane, row,
        )
        for i, v in enumerate(values):
            put(t, i, v)

    @pl.loop(1, 7)
    def _(t):
        for i in range(NMSG):
            put(t, i, inner[t - 1, i])


def middle_kernel(force_ref, r1, r1h, r2_hbm, r2, sem):
    lane, row = lanes(), rows()
    force = force_of(force_ref)

    def copy(t):
        return pltpu.make_async_copy(r2.at[t], r2_hbm.at[t], sem.at[t])

    def step(t):
        def get(k, s, p):
            return r1h[k, 8 * p : 8 * p + 8, :] if s is None else r1[k, s, 8 * p : 8 * p + 8, :]

        for p in range(4):
            g = collide(stream_own(get, None, p, t, lane, row), force)
            for k in range(19):
                r2[t, k, 8 * p : 8 * p + 8, :] = g[k]
        copy(t).start()

    for t in (0, 7, 8):
        step(t)

    @pl.loop(1, 7)
    def _(t):
        step(t)

    for t in range(9):
        copy(t).wait()


def last_kernel(
    force_ref, r2_hbm, edge, far, near, mask, density, velocity, r2, r3, got, r2h, r2e, r3h, sem
):
    copy = pltpu.make_async_copy(r2_hbm, r2, sem)
    copy.start()

    def load2(k, s, p):
        return r2[s, k, 8 * p : 8 * p + 8, :]

    def load3(k, s, p):
        return r3[s, k, 8 * p : 8 * p + 8, :]

    lane, row = lanes(), rows()
    force = force_of(force_ref)
    force_rim = rim_force(force, row)
    even_y = lax.rem(lax.axis_index("gy"), 2) == 0

    @pl.loop(0, 9)
    def _(t):
        for i in range(NMSG):
            v = jnp.concatenate([near[i, t], far[i, t]], axis=0)
            got[i, t] = jnp.where(even_y, pltpu.roll(v, 4, axis=0), v)

    copy.wait()

    @pl.loop(0, 9)
    def _(t):
        f = [None] * 19
        for i, k in enumerate(LOCAL):
            f[k] = edge[5 + i, t]
        for i, k in enumerate(IN):
            own = edge[OUT.index(OPP[k]), t]
            f[k] = stream_rim(lambda s, i=i: got[i, s], own, k, t, lane, row)
        g = collide(f, force_rim)
        for k in range(19):
            r2[t, k, pl.ds(0, 4, stride=8), :] = g[k][0:4]
            r2[t, FLIP[k], pl.ds(7, 4, stride=8), :] = g[k][4:8]
        for i, k in enumerate(OUT):
            r2e[i, t] = g[k]
        f = [None] * 19
        for i, k in enumerate(LOCAL):
            f[FLIP[k]] = got[5 + i, t]
        for i, k in enumerate(OUT):
            own = got[IN.index(OPP[k]), t]
            f[k] = stream_rim(lambda s, i=i: edge[i, s], own, k, t, lane, row)
        g = collide(f, force_rim)
        for i, k in enumerate(IN + FLAT + OUT):
            r2h[i, t] = g[k]

    place = {k: i for i, k in enumerate(IN + FLAT + OUT)}

    @pl.loop(0, 9)
    def _(t):
        f = [None] * 19
        for k in range(19):
            own = r2h[place[OPP[k]], t]
            if k == 0:
                f[k] = own
            elif k in FLAT:
                f[k] = stream_rim(lambda s, k=k: r2h[place[k], s], own, k, t, lane, row)
            elif k in IN:
                f[k] = stream_rim(lambda s, k=k: got[19 + IN.index(k), s], own, k, t, lane, row)
            else:
                f[k] = stream_rim(lambda s, k=k: r2e[OUT.index(k), s], own, k, t, lane, row)
        g = collide(f, force_rim)
        for i, k in enumerate(IN):
            r3h[i, t] = g[k]
        for p in range(4):
            g = collide(stream_own(load2, r2h, p, t, lane, row), force)
            for k in range(19):
                r3[t, k, 8 * p : 8 * p + 8, :] = g[k]

    @pl.loop(0, 8)
    def _(t):
        at = pl.ds(pl.multiple_of(t * 128, 128), 128)
        for p in range(4):
            f = stream_own(load3, r3h, p, t, lane, row)
            rho = f[0]
            for k in range(1, 19):
                rho = rho + f[k]
            solid = mask[p, :, at] > 0
            density[p, :, at] = jnp.where(solid, 0.0, rho)
            inv = (1.0 / MACH) / rho
            for a in range(3):
                plus = [f[k] for k in range(19) if VEL[k][a] == 1]
                minus = [f[k] for k in range(19) if VEL[k][a] == -1]
                j = plus[0] - minus[0]
                for x, y in zip(plus[1:], minus[1:]):
                    j = j + (x - y)
                velocity[a, p, :, at] = jnp.where(solid, 0.0, j * inv)


VMEM = pl.BlockSpec(memory_space=pltpu.VMEM)
SMEM = pl.BlockSpec(memory_space=pltpu.SMEM)
HBM = pl.BlockSpec(memory_space=pltpu.HBM)


def call(kernel, name, us, out_shape, in_specs, out_specs, scratch, room=40):
    return pl.pallas_call(
        kernel,
        out_shape=out_shape,
        in_specs=in_specs,
        out_specs=out_specs,
        scratch_shapes=scratch,
        compiler_params=pltpu.CompilerParams(vmem_limit_bytes=room * 1024 * 1024),
        cost_estimate=pl.CostEstimate(
            flops=int(us * 1e6), bytes_accessed=int(us * 3e6), transcendentals=0
        ),
        name=name,
    )


def sds(*shape):
    return jax.ShapeDtypeStruct(shape, F32)


def buf(*shape):
    return pltpu.VMEM(shape, F32)


def swap(x, axis, parity):
    count = lax.axis_size(axis)
    pairs = [(i, (i + 1) % count if i % 2 == parity else (i - 1) % count) for i in range(count)]
    return lax.ppermute(x, axis, pairs)


def local(pop, mask, force):
    far_memory = [pltpu.with_memory_space_constraint(x, pltpu.HBM) for x in (pop, mask)]
    z1, z0 = call(
        pack_kernel, "pack", 0.7,
        (sds(3, 8, 128), sds(3, 8, 128)), [HBM, HBM], (VMEM, VMEM),
        [buf(19, 4, 8, 128), buf(19, 4, 8, 128), pltpu.VMEM((4, 8, 128), jnp.int32),
         pltpu.VMEM((4, 8, 128), jnp.int32), pltpu.SemaphoreType.DMA((10,))],
    )(*far_memory)
    got1 = swap(z1, "gz", 1)
    got0 = swap(z0, "gz", 0)
    r1, e1, e2, e3, inner = call(
        collide_kernel, "collide", 3.0,
        (sds(19, 8, 32, 128), sds(8, 19, 8, 128), sds(8, 19, 8, 128), sds(8, 5, 8, 128),
         sds(6, NMSG, 8, 128)),
        [SMEM, VMEM, VMEM], (VMEM,) * 5, [],
    )(force, pop, mask)
    r1h, edge, far, near = call(
        rim_kernel, "rim", 1.0,
        (sds(19, 32, 128), sds(NMSG, 9, 8, 128), sds(NMSG, 9, 4, 128), sds(NMSG, 9, 4, 128)),
        [SMEM] + [VMEM] * 6, (VMEM,) * 4,
        [buf(19, 4, 8, 128), buf(19, 8, 128), buf(19, 8, 128), buf(5, 8, 128)],
    )(force, e1, e2, e3, inner, got1, got0)
    far = swap(far, "gy", 1)
    near = swap(near, "gy", 0)
    r2 = call(
        middle_kernel, "middle", 3.0,
        sds(9, 19, 32, 128), [SMEM, VMEM, VMEM], HBM,
        [buf(9, 19, 32, 128), pltpu.SemaphoreType.DMA((9,))],
    )(force, r1, r1h)
    return call(
        last_kernel, "last", 5.0,
        (sds(4, 8, 1024), sds(3, 4, 8, 1024)),
        [SMEM, HBM, VMEM, VMEM, VMEM, VMEM], (VMEM, VMEM),
        [buf(9, 19, 32, 128), buf(9, 19, 32, 128), buf(NMSG, 9, 8, 128), buf(19, 9, 8, 128),
         buf(5, 9, 8, 128), buf(5, 9, 8, 128), pltpu.SemaphoreType.DMA],
    )(force, r2, edge, far, near, mask)


def solution(mesh):
    return jax.shard_map(
        local,
        mesh=mesh,
        in_specs=(P(None, None, "gy", "gz"), P(None, "gy", "gz"), P()),
        out_specs=(P(None, "gy", "gz"), P(None, None, "gy", "gz")),
        check_vma=False,
    )
```

```python
import jax
import jax.numpy as jnp
from jax import lax
from jax.experimental import pallas as pl
from jax.experimental.pallas import tpu as pltpu
from jax.sharding import PartitionSpec as P

VEL = [
    (0, 0, 0),
    (1, 0, 0),
    (-1, 0, 0),
    (0, 1, 0),
    (0, -1, 0),
    (0, 0, 1),
    (0, 0, -1),
    (1, 1, 0),
    (-1, -1, 0),
    (1, -1, 0),
    (-1, 1, 0),
    (1, 0, 1),
    (-1, 0, -1),
    (1, 0, -1),
    (-1, 0, 1),
    (0, 1, 1),
    (0, -1, -1),
    (0, 1, -1),
    (0, -1, 1),
]
OPP = [VEL.index((-x, -y, -z)) for x, y, z in VEL]
FLIP = [VEL.index((x, -y, z)) for x, y, z in VEL]
IN = [k for k in range(19) if VEL[k][1] == 1]
OUT = [FLIP[k] for k in IN]
FLAT = [k for k in range(19) if VEL[k][1] == 0]
LOCAL = FLAT + OUT
NMSG = 24
MACH = 0.05
BIG = 1e30
NAN = float("nan")
F32 = jnp.float32


def lanes():
    return lax.broadcasted_iota(jnp.int32, (8, 128), 1)


def rows():
    return lax.broadcasted_iota(jnp.int32, (8, 128), 0)


def collide(f, force):
    fx, fy, fz = force
    sx, dx = f[1] + f[2], f[1] - f[2]
    sy, dy = f[3] + f[4], f[3] - f[4]
    sz, dz = f[5] + f[6], f[5] - f[6]

    def plane(a):
        big, small = f[a] + f[a + 1], f[a] - f[a + 1]
        big2, small2 = f[a + 2] + f[a + 3], f[a + 2] - f[a + 3]
        return big + big2, big - big2, small + small2, small - small2, (small, small2)

    nxy, mxy, tyyx, txxy, odd_xy = plane(7)
    nxz, mxz, tzzx, txxz, odd_xz = plane(11)
    nyz, myz, tzzy, tyyz, odd_yz = plane(15)
    tx, ty, tz = tyyx + tzzx, txxy + tzzy, txxz + tyyz
    jx, jy, jz = dx + tx, dy + ty, dz + tz
    nx, ny, nz = nxy + nxz, nxy + nyz, nxz + nyz
    total_s = (sx + sy) + sz
    total_n = nx + nyz
    rho = (f[0] + total_s) + total_n
    inv = 0.3125 / rho
    vx, vy, vz = jx * inv, jy * inv, jz * inv
    gx, gy, gz = jx * vx, jy * vy, jz * vz
    total_g = (gx + gy) + gz
    mxy = jx * vy - 0.0625 * mxy
    mxz = jx * vz - 0.0625 * mxz
    myz = jy * vz - 0.0625 * myz
    base = rho * (1.3 / 36.0) + total_g * (1.3 / 3.75)
    nxy = (base - 0.52 * gz) - 0.075 * nxy
    nxz = (base - 0.52 * gy) - 0.075 * nxz
    nyz = (base - 0.52 * gx) - 0.075 * nyz
    bx = jx * (0.4 / 3.0) + fx * (1.0 / 12.0)
    by = jy * (0.4 / 3.0) + fy * (1.0 / 12.0)
    bz = jz * (0.4 / 3.0) + fz * (1.0 / 12.0)
    rest = rho * (1.25 / 6.0 - 5.2 / 36.0) + total_g * (1.04 - 5.2 / 3.75)
    out = [None] * 19

    def axis(a, g, s, n, d, t, force_a):
        even = ((rest + 0.96 * g) - 0.125 * s) + 0.025 * n
        odd = (0.8 / 3.0 * t - 0.1 / 3.0 * d) + force_a * (1.0 / 6.0)
        out[a], out[a + 1] = even + odd, even - odd

    def edge(a, n, m, b1, b2, p, q):
        big, big2 = n + m, n - m
        small, small2 = (b1 + b2) - 0.3 * p, (b1 - b2) - 0.3 * q
        out[a], out[a + 1] = big + small, big - small
        out[a + 2], out[a + 3] = big2 + small2, big2 - small2

    axis(1, gx, sx, nx, dx, tx, fx)
    axis(3, gy, sy, ny, dy, ty, fy)
    axis(5, gz, sz, nz, dz, tz, fz)
    edge(7, nxy, mxy, bx, by, *odd_xy)
    edge(11, nxz, mxz, bx, bz, *odd_xz)
    edge(15, nyz, myz, by, bz, *odd_yz)
    out[0] = (rho * (1.0 - 1.25 + 15.6 / 36.0) + total_g * (15.6 / 3.75 - 6.08)) + (
        0.25 * total_s + 0.2 * total_n
    )
    return out


def along_z(get, t, cz, lane, split=False):
    def at(s):
        return get(None if split and s == 8 else s)

    if isinstance(t, int):
        prev, succ = (t + 8) % 9, (t + 1) % 9
    elif split:
        prev, succ = t - 1, t + 1
    else:
        prev, succ = jnp.where(t == 0, 8, t - 1), jnp.where(t == 8, 0, t + 1)
    cur = at(t) if isinstance(t, int) else get(t)
    if cz == 0:
        return cur
    if cz == 1:
        before = at(prev) if isinstance(t, int) else get(prev)
        return pltpu.roll(jnp.where(lane == 127, before, cur), 1, axis=1)
    after = at(succ) if isinstance(t, int) else get(succ)
    return pltpu.roll(jnp.where(lane == 0, after, cur), 127, axis=1)


def stream_own(load, p, t, lane, split=False):
    f = []
    for k in range(19):
        cx, cy, cz = VEL[k]
        own = load(OPP[k], None if split and isinstance(t, int) and t == 8 else t, p, 0)
        q = p - cx
        if k == 0 or q < 0 or q > 3:
            f.append(own)
            continue
        v = along_z(lambda s, k=k, q=q, cy=cy: load(k, s, q, cy), t, cz, lane, split)
        f.append(jnp.where(v < BIG, v, own))
    return f


def stream_rim(get, own, k, t, lane, row):
    cx, _, cz = VEL[k]
    v = along_z(get, t, cz, lane)
    if cx:
        v = pltpu.roll(v, cx % 8, axis=0)
        wall = (row & 3) == (0 if cx == 1 else 3)
        v = jnp.where(wall, NAN, v)
    return jnp.where(v < BIG, v, own)


def edges(ref, flipped, lower, upper):
    a = ref[pl.ds(lower, 4, stride=8), :]
    b = flipped[pl.ds(upper, 4, stride=8), :]
    return jnp.concatenate([a, b], axis=0)


def force_of(force_ref):
    return force_ref[0], force_ref[1], force_ref[2]


def rim_force(force, row):
    fx, fy, fz = force
    return fx, jnp.where(row < 4, fy, -fy), fz


GROUPS = ((0, 5), (5, 10), (10, 15), (15, 19))


def pack_kernel(pop_hbm, mask_hbm, out1, out0, first, last, mask_first, mask_last, sem):
    copies = [
        pltpu.make_async_copy(mask_hbm.at[:, :, 0:128], mask_first, sem.at[0]),
        pltpu.make_async_copy(mask_hbm.at[:, :, 896:1024], mask_last, sem.at[1]),
    ]
    for i, (a, b) in enumerate(GROUPS):
        for j, (at, to) in enumerate(((0, first), (896, last))):
            copies.append(
                pltpu.make_async_copy(
                    pop_hbm.at[a:b, :, :, at : at + 128], to.at[a:b], sem.at[2 + 2 * i + j]
                )
            )
    for copy in copies:
        copy.start()
    for copy in copies:
        copy.wait()
    lane = lanes()
    even = lax.rem(lax.axis_index("gz"), 2) == 0
    group = lane // 4
    for tile in range(3):
        left = jnp.zeros((8, 128), F32)
        right = jnp.zeros((8, 128), F32)
        for s in range(32):
            i = tile * 32 + s
            if i >= 76:
                break
            k, p = i // 4, i % 4
            a, b = first[k, p], last[k, p]
            if k == 0:
                a = jnp.where(mask_first[p] > 0, NAN, a)
                b = jnp.where(mask_last[p] > 0, NAN, b)
            if s:
                a = pltpu.roll(a, 4 * s, axis=1)
            if s != 31:
                b = pltpu.roll(b, 4 * s + 4, axis=1)
            left = jnp.where(group == s, a, left)
            right = jnp.where(group == s, b, right)
        out0[tile] = jnp.where(even, right, left)
        out1[tile] = jnp.where(even, left, right)


def rim_values(e1, e2, e3, t, force_rim, lane, row):
    own = [e1(k, t) for k in range(19)]
    values = [own[k] for k in OUT]
    for k in LOCAL:
        if k == 0:
            values.append(own[0])
        else:
            src = e1 if k in FLAT else e2
            values.append(stream_rim(lambda s, k=k, src=src: src(k, s), own[OPP[k]], k, t, lane, row))
    own = [e2(k, t) for k in range(19)]
    f = [own[0]]
    for k in range(1, 19):
        src = e2 if k in FLAT else (e1 if k in IN else e3)
        f.append(stream_rim(lambda s, k=k, src=src: src(k, s), own[OPP[k]], k, t, lane, row))
    g = collide(f, force_rim)
    return values + [g[k] for k in OUT]


def collide_kernel(force_ref, pop, mask, r1, e1, e2, e3, inner):
    lane, row = lanes(), rows()
    force = force_of(force_ref)
    force_rim = rim_force(force, row)

    @pl.loop(0, 8, unroll=8)
    def _(t):
        at = pl.ds(pl.multiple_of(t * 128, 128), 128)
        for p in range(4):
            f = [pop[k, p, :, at] for k in range(19)]
            f[0] = jnp.where(mask[p, :, at] > 0, NAN, f[0])
            g = collide(f, force)
            for k in range(19):
                r1[k, t, 8 * p : 8 * p + 8, :] = g[k]
        for k in range(19):
            e1[t, k] = edges(r1.at[k, t], r1.at[FLIP[k], t], 0, 7)
            e2[t, k] = edges(r1.at[k, t], r1.at[FLIP[k], t], 1, 6)
        for i, k in enumerate(OUT):
            e3[t, i] = edges(r1.at[k, t], r1.at[FLIP[k], t], 2, 5)

    @pl.loop(1, 7, unroll=6)
    def _(t):
        values = rim_values(
            lambda k, s: e1[s, k], lambda k, s: e2[s, k], lambda k, s: e3[s, OUT.index(k)],
            t, force_rim, lane, row,
        )
        for i, v in enumerate(values):
            inner[t - 1, i] = v


def rim_kernel(force_ref, e1, e2, e3, inner, got1, got0, r1h, edge, far, near, strip, h1, h2, h3):
    lane, row = lanes(), rows()
    force = force_of(force_ref)
    force_rim = rim_force(force, row)
    even_z = lax.rem(lax.axis_index("gz"), 2) == 0
    even_y = lax.rem(lax.axis_index("gy"), 2) == 0
    for tile in range(3):
        a, b = got0[tile], got1[tile]
        from_right = jnp.where(even_z, a, b)
        from_left = jnp.where(even_z, b, a)
        for s in range(32):
            i = tile * 32 + s
            if i >= 76:
                break
            k, p = i // 4, i % 4
            x = pltpu.roll(from_right, 128 - 4 * s, axis=1) if s else from_right
            y = pltpu.roll(from_left, 124 - 4 * s, axis=1) if s != 31 else from_left
            strip[k, p] = jnp.where(lane < 64, x, y)
    for p in range(4):
        g = collide([strip[k, p] for k in range(19)], force)
        for k in range(19):
            r1h[k, 8 * p : 8 * p + 8, :] = g[k]
    for k in range(19):
        h1[k] = edges(r1h.at[k], r1h.at[FLIP[k]], 0, 7)
        h2[k] = edges(r1h.at[k], r1h.at[FLIP[k]], 1, 6)
    for i, k in enumerate(OUT):
        h3[i] = edges(r1h.at[k], r1h.at[FLIP[k]], 2, 5)

    def put(t, i, v):
        edge[i, t] = v
        w = jnp.where(even_y, pltpu.roll(v, 4, axis=0), v)
        near[i, t] = w[0:4]
        far[i, t] = w[4:8]

    for t in (0, 7, 8):
        values = rim_values(
            lambda k, s: h1[k] if s == 8 else e1[s, k],
            lambda k, s: h2[k] if s == 8 else e2[s, k],
            lambda k, s: h3[OUT.index(k)] if s == 8 else e3[s, OUT.index(k)],
            t, force_rim, lane, row,
        )
        for i, v in enumerate(values):
            put(t, i, v)

    @pl.loop(1, 7, unroll=6)
    def _(t):
        for i in range(NMSG):
            put(t, i, inner[t - 1, i])


def middle_kernel(force_ref, r1, r1h, r2):
    lane = lanes()
    force = force_of(force_ref)

    def step(t):
        def get(k, s, p, cy):
            v = r1h[k, 8 * p : 8 * p + 8, :] if s is None else r1[k, s, 8 * p : 8 * p + 8, :]
            return pltpu.roll(v, cy % 8, axis=0) if cy else v

        for p in range(4):
            g = collide(stream_own(get, p, t, lane, split=True), force)
            for k in range(19):
                r2[t, k, 8 * p : 8 * p + 8, :] = g[k]

    for t in (0, 7, 8):
        step(t)

    @pl.loop(1, 7)
    def _(t):
        step(t)


def last_kernel(
    force_ref, r2_in, edge, far, near, mask, density, velocity, r2, r3, got, got2, r2h, r2e
):
    def load2(k, s, p, cy):
        return r2[s, k, pl.ds(10 * p + 1 - cy, 8), :]

    def load3(k, s, p, cy):
        return r3[s, k, pl.ds(10 * p + 1 - cy, 8), :]

    def around(ref, t, k, v):
        ref[t, k, pl.ds(0, 4, stride=10), :] = v[0:4]
        ref[t, FLIP[k], pl.ds(9, 4, stride=10), :] = v[4:8]

    lane, row = lanes(), rows()
    force = force_of(force_ref)
    force_rim = rim_force(force, row)
    even_y = lax.rem(lax.axis_index("gy"), 2) == 0

    def received(i, t):
        v = jnp.concatenate([near[i, t], far[i, t]], axis=0)
        return jnp.where(even_y, pltpu.roll(v, 4, axis=0), v)

    @pl.loop(0, 9, unroll=9)
    def _(t):
        for i in range(5):
            got[i, t] = received(i, t)

    @pl.loop(0, 9, unroll=9)
    def _(t):
        for k in range(19):
            for p in range(4):
                r2[t, k, pl.ds(10 * p + 1, 8), :] = r2_in[t, k, 8 * p : 8 * p + 8, :]
        f = [None] * 19
        for i, k in enumerate(LOCAL):
            f[k] = edge[5 + i, t]
        for i, k in enumerate(IN):
            own = edge[OUT.index(OPP[k]), t]
            f[k] = stream_rim(lambda s, i=i: got[i, s], own, k, t, lane, row)
        g = collide(f, force_rim)
        for k in range(19):
            r2[t, k, pl.ds(1, 4, stride=10), :] = g[k][0:4]
            r2[t, FLIP[k], pl.ds(8, 4, stride=10), :] = g[k][4:8]
        for i, k in enumerate(OUT):
            r2e[i, t] = g[k]
        f = [None] * 19
        for i, k in enumerate(LOCAL):
            f[FLIP[k]] = received(5 + i, t)
        for i, k in enumerate(OUT):
            own = got[IN.index(OPP[k]), t]
            f[k] = stream_rim(lambda s, i=i: edge[i, s], own, k, t, lane, row)
        g = collide(f, force_rim)
        for i, k in enumerate(IN + FLAT + OUT):
            r2h[i, t] = g[k]
            if k in IN:
                around(r2, t, k, g[k])
        for i in range(5):
            got2[i, t] = received(19 + i, t)

    place = {k: i for i, k in enumerate(IN + FLAT + OUT)}

    @pl.loop(0, 9, unroll=9)
    def _(t):
        f = [None] * 19
        for k in range(19):
            own = r2h[place[OPP[k]], t]
            if k == 0:
                f[k] = own
            elif k in FLAT:
                f[k] = stream_rim(lambda s, k=k: r2h[place[k], s], own, k, t, lane, row)
            elif k in IN:
                f[k] = stream_rim(lambda s, k=k: got2[IN.index(k), s], own, k, t, lane, row)
            else:
                f[k] = stream_rim(lambda s, k=k: r2e[OUT.index(k), s], own, k, t, lane, row)
        g = collide(f, force_rim)
        for k in IN:
            around(r3, t, k, g[k])
        for p in range(4):
            g = collide(stream_own(load2, p, t, lane), force)
            for k in range(19):
                r3[t, k, pl.ds(10 * p + 1, 8), :] = g[k]

    @pl.loop(0, 8, unroll=8)
    def _(t):
        at = pl.ds(pl.multiple_of(t * 128, 128), 128)
        for p in range(4):
            f = stream_own(load3, p, t, lane)
            rho = f[0]
            for k in range(1, 19):
                rho = rho + f[k]
            solid = mask[p, :, at] > 0
            density[p, :, at] = jnp.where(solid, 0.0, rho)
            inv = (1.0 / MACH) / rho
            for a in range(3):
                plus = [f[k] for k in range(19) if VEL[k][a] == 1]
                minus = [f[k] for k in range(19) if VEL[k][a] == -1]
                j = plus[0] - minus[0]
                for x, y in zip(plus[1:], minus[1:]):
                    j = j + (x - y)
                velocity[a, p, :, at] = jnp.where(solid, 0.0, j * inv)


VMEM = pl.BlockSpec(memory_space=pltpu.VMEM)
SMEM = pl.BlockSpec(memory_space=pltpu.SMEM)
HBM = pl.BlockSpec(memory_space=pltpu.HBM)


def call(kernel, name, us, out_shape, in_specs, out_specs, scratch, room=40):
    return pl.pallas_call(
        kernel,
        out_shape=out_shape,
        in_specs=in_specs,
        out_specs=out_specs,
        scratch_shapes=scratch,
        compiler_params=pltpu.CompilerParams(vmem_limit_bytes=room * 1024 * 1024),
        cost_estimate=pl.CostEstimate(
            flops=int(us * 1e6), bytes_accessed=int(us * 3e6), transcendentals=0
        ),
        name=name,
    )


def sds(*shape):
    return jax.ShapeDtypeStruct(shape, F32)


def buf(*shape):
    return pltpu.VMEM(shape, F32)


def swap(x, axis, parity):
    count = lax.axis_size(axis)
    pairs = [(i, (i + 1) % count if i % 2 == parity else (i - 1) % count) for i in range(count)]
    return lax.ppermute(x, axis, pairs)


def local(pop, mask, force):
    far_memory = [pltpu.with_memory_space_constraint(x, pltpu.HBM) for x in (pop, mask)]
    z1, z0 = call(
        pack_kernel, "pack", 0.7,
        (sds(3, 8, 128), sds(3, 8, 128)), [HBM, HBM], (VMEM, VMEM),
        [buf(19, 4, 8, 128), buf(19, 4, 8, 128), pltpu.VMEM((4, 8, 128), jnp.int32),
         pltpu.VMEM((4, 8, 128), jnp.int32), pltpu.SemaphoreType.DMA((10,))],
    )(*far_memory)
    got1 = swap(z1, "gz", 1)
    got0 = swap(z0, "gz", 0)
    r1, e1, e2, e3, inner = call(
        collide_kernel, "collide", 3.0,
        (sds(19, 8, 32, 128), sds(8, 19, 8, 128), sds(8, 19, 8, 128), sds(8, 5, 8, 128),
         sds(6, NMSG, 8, 128)),
        [SMEM, VMEM, VMEM], (VMEM,) * 5, [],
    )(force, pop, mask)
    r1h, edge, far, near = call(
        rim_kernel, "rim", 1.0,
        (sds(19, 32, 128), sds(NMSG, 9, 8, 128), sds(NMSG, 9, 4, 128), sds(NMSG, 9, 4, 128)),
        [SMEM] + [VMEM] * 6, (VMEM,) * 4,
        [buf(19, 4, 8, 128), buf(19, 8, 128), buf(19, 8, 128), buf(5, 8, 128)],
    )(force, e1, e2, e3, inner, got1, got0)
    far = swap(far, "gy", 1)
    near = swap(near, "gy", 0)
    r2 = call(
        middle_kernel, "middle", 3.0,
        sds(9, 19, 32, 128), [SMEM, VMEM, VMEM], VMEM, [],
    )(force, r1, r1h)
    return call(
        last_kernel, "last", 5.0,
        (sds(4, 8, 1024), sds(3, 4, 8, 1024)),
        [SMEM] + [VMEM] * 5, (VMEM, VMEM),
        [buf(9, 19, 40, 128), buf(9, 19, 40, 128), buf(5, 9, 8, 128), buf(5, 9, 8, 128),
         buf(19, 9, 8, 128), buf(5, 9, 8, 128)],
    )(force, r2, edge, far, near, mask)


def solution(mesh):
    return jax.shard_map(
        local,
        mesh=mesh,
        in_specs=(P(None, None, "gy", "gz"), P(None, "gy", "gz"), P()),
        out_specs=(P(None, "gy", "gz"), P(None, None, "gy", "gz")),
        check_vma=False,
    )
```

```python
import jax
import jax.numpy as jnp
from jax import lax
from jax.experimental import pallas as pl
from jax.experimental.pallas import tpu as pltpu
from jax.sharding import PartitionSpec as P

VEL = [
    (0, 0, 0),
    (1, 0, 0),
    (-1, 0, 0),
    (0, 1, 0),
    (0, -1, 0),
    (0, 0, 1),
    (0, 0, -1),
    (1, 1, 0),
    (-1, -1, 0),
    (1, -1, 0),
    (-1, 1, 0),
    (1, 0, 1),
    (-1, 0, -1),
    (1, 0, -1),
    (-1, 0, 1),
    (0, 1, 1),
    (0, -1, -1),
    (0, 1, -1),
    (0, -1, 1),
]
OPP = [VEL.index((-x, -y, -z)) for x, y, z in VEL]
FLIP = [VEL.index((x, -y, z)) for x, y, z in VEL]
IN = [k for k in range(19) if VEL[k][1] == 1]
OUT = [FLIP[k] for k in IN]
FLAT = [k for k in range(19) if VEL[k][1] == 0]
LOCAL = FLAT + OUT
NMSG = 24
MACH = 0.05
BIG = 1e30
NAN = float("nan")
F32 = jnp.float32


def lanes():
    return lax.broadcasted_iota(jnp.int32, (8, 128), 1)


def rows():
    return lax.broadcasted_iota(jnp.int32, (8, 128), 0)


def collide(f, force):
    fx, fy, fz = force
    sx, dx = f[1] + f[2], f[1] - f[2]
    sy, dy = f[3] + f[4], f[3] - f[4]
    sz, dz = f[5] + f[6], f[5] - f[6]

    def plane(a):
        big, small = f[a] + f[a + 1], f[a] - f[a + 1]
        big2, small2 = f[a + 2] + f[a + 3], f[a + 2] - f[a + 3]
        return big + big2, big - big2, small + small2, small - small2, (small, small2)

    nxy, mxy, tyyx, txxy, odd_xy = plane(7)
    nxz, mxz, tzzx, txxz, odd_xz = plane(11)
    nyz, myz, tzzy, tyyz, odd_yz = plane(15)
    tx, ty, tz = tyyx + tzzx, txxy + tzzy, txxz + tyyz
    jx, jy, jz = dx + tx, dy + ty, dz + tz
    nx, ny, nz = nxy + nxz, nxy + nyz, nxz + nyz
    total_s = (sx + sy) + sz
    total_n = nx + nyz
    rho = (f[0] + total_s) + total_n
    inv = 0.3125 / rho
    vx, vy, vz = jx * inv, jy * inv, jz * inv
    gx, gy, gz = jx * vx, jy * vy, jz * vz
    total_g = (gx + gy) + gz
    mxy = jx * vy - 0.0625 * mxy
    mxz = jx * vz - 0.0625 * mxz
    myz = jy * vz - 0.0625 * myz
    base = rho * (1.3 / 36.0) + total_g * (1.3 / 3.75)
    nxy = (base - 0.52 * gz) - 0.075 * nxy
    nxz = (base - 0.52 * gy) - 0.075 * nxz
    nyz = (base - 0.52 * gx) - 0.075 * nyz
    bx = jx * (0.4 / 3.0) + fx * (1.0 / 12.0)
    by = jy * (0.4 / 3.0) + fy * (1.0 / 12.0)
    bz = jz * (0.4 / 3.0) + fz * (1.0 / 12.0)
    rest = rho * (1.25 / 6.0 - 5.2 / 36.0) + total_g * (1.04 - 5.2 / 3.75)
    out = [None] * 19

    def axis(a, g, s, n, d, t, force_a):
        even = ((rest + 0.96 * g) - 0.125 * s) + 0.025 * n
        odd = (0.8 / 3.0 * t - 0.1 / 3.0 * d) + force_a * (1.0 / 6.0)
        out[a], out[a + 1] = even + odd, even - odd

    def edge(a, n, m, b1, b2, p, q):
        big, big2 = n + m, n - m
        small, small2 = (b1 + b2) - 0.3 * p, (b1 - b2) - 0.3 * q
        out[a], out[a + 1] = big + small, big - small
        out[a + 2], out[a + 3] = big2 + small2, big2 - small2

    axis(1, gx, sx, nx, dx, tx, fx)
    axis(3, gy, sy, ny, dy, ty, fy)
    axis(5, gz, sz, nz, dz, tz, fz)
    edge(7, nxy, mxy, bx, by, *odd_xy)
    edge(11, nxz, mxz, bx, bz, *odd_xz)
    edge(15, nyz, myz, by, bz, *odd_yz)
    out[0] = (rho * (1.0 - 1.25 + 15.6 / 36.0) + total_g * (15.6 / 3.75 - 6.08)) + (
        0.25 * total_s + 0.2 * total_n
    )
    return out


def along_z(get, t, cz, lane):
    cur = get(t)
    if cz == 0:
        return cur
    if cz == 1:
        before = get((t + 8) % 9 if isinstance(t, int) else jnp.where(t == 0, 8, t - 1))
        return pltpu.roll(jnp.where(lane == 127, before, cur), 1, axis=1)
    after = get((t + 1) % 9 if isinstance(t, int) else jnp.where(t == 8, 0, t + 1))
    return pltpu.roll(jnp.where(lane == 0, after, cur), 127, axis=1)


def stream_own(load, p, t, lane):
    f = []
    for k in range(19):
        cx, cy, cz = VEL[k]
        own = load(OPP[k], t, p, 0)
        q = p - cx
        if k == 0 or q < 0 or q > 3:
            f.append(own)
            continue
        v = along_z(lambda s, k=k, q=q, cy=cy: load(k, s, q, cy), t, cz, lane)
        f.append(jnp.where(v < BIG, v, own))
    return f


def stream_rim(get, own, k, t, lane, row):
    cx, _, cz = VEL[k]
    v = along_z(get, t, cz, lane)
    if cx:
        v = pltpu.roll(v, cx % 8, axis=0)
        wall = (row & 3) == (0 if cx == 1 else 3)
        v = jnp.where(wall, NAN, v)
    return jnp.where(v < BIG, v, own)


def edges(ref, flipped, lower, upper):
    a = ref[pl.ds(lower, 4, stride=8), :]
    b = flipped[pl.ds(upper, 4, stride=8), :]
    return jnp.concatenate([a, b], axis=0)


def force_of(force_ref):
    return force_ref[0], force_ref[1], force_ref[2]


def rim_force(force, row):
    fx, fy, fz = force
    return fx, jnp.where(row < 4, fy, -fy), fz


GROUPS = ((0, 10), (10, 19))


def pack_kernel(pop_hbm, mask_hbm, force_hbm, out1, out0, mask, force, first, last, given, sem):
    copies = [
        pltpu.make_async_copy(mask_hbm, mask, sem.at[0]),
        pltpu.make_async_copy(force_hbm, given, sem.at[1]),
    ]
    for i, (a, b) in enumerate(GROUPS):
        for j, (at, to) in enumerate(((0, first), (896, last))):
            copies.append(
                pltpu.make_async_copy(
                    pop_hbm.at[a:b, :, :, at : at + 128], to.at[a:b], sem.at[2 + 2 * i + j]
                )
            )
    for copy in copies:
        copy.start()
    copies[0].wait()
    copies[1].wait()
    for i in range(3):
        force[i] = jnp.full((8, 128), given[i], F32)
    lane = lanes()
    even = lax.rem(lax.axis_index("gz"), 2) == 0
    group = lane // 8
    left = [jnp.zeros((8, 128), F32)] * 5
    right = [jnp.zeros((8, 128), F32)] * 5
    for n, (k0, k1) in enumerate(GROUPS):
        copies[2 + 2 * n].wait()
        copies[3 + 2 * n].wait()
        for k in range(k0, k1):
            for p in range(4):
                tile, s = divmod(4 * k + p, 16)
                a, b = first[k, p], last[k, p]
                if k == 0:
                    a = jnp.where(mask[p, :, 0:128] > 0, NAN, a)
                    b = jnp.where(mask[p, :, 896:1024] > 0, NAN, b)
                if s:
                    a = pltpu.roll(a, 8 * s, axis=1)
                    b = pltpu.roll(b, 8 * s, axis=1)
                left[tile] = jnp.where(group == s, a, left[tile])
                right[tile] = jnp.where(group == (s + 15) % 16, b, right[tile])
    for tile in range(5):
        out0[tile] = jnp.where(even, right[tile], left[tile])
        out1[tile] = jnp.where(even, left[tile], right[tile])


def rim_values(e1, e2, e3, t, force_rim, lane, row):
    own = [e1(k, t) for k in range(19)]
    values = [own[k] for k in OUT]
    for k in LOCAL:
        if k == 0:
            values.append(own[0])
        else:
            src = e1 if k in FLAT else e2
            values.append(stream_rim(lambda s, k=k, src=src: src(k, s), own[OPP[k]], k, t, lane, row))
    own = [e2(k, t) for k in range(19)]
    f = [own[0]]
    for k in range(1, 19):
        src = e2 if k in FLAT else (e1 if k in IN else e3)
        f.append(stream_rim(lambda s, k=k, src=src: src(k, s), own[OPP[k]], k, t, lane, row))
    g = collide(f, force_rim)
    return values + [g[k] for k in OUT]


def edge_kernel(force_ref, pop, mask, e1, e2, e3, inner):
    lane, row = lanes(), rows()
    force_rim = rim_force(force_of(force_ref), row)

    def take(k, t, lower, upper):
        a = pop[k, pl.ds(8 * t + lower, 4, stride=64), :]
        b = pop[FLIP[k], pl.ds(8 * t + upper, 4, stride=64), :]
        return jnp.concatenate([a, b], axis=0)

    for t in range(8):
        for depth, e in enumerate((e1, e2, e3)):
            f = [take(k, t, depth, 7 - depth) for k in range(19)]
            a = mask[pl.ds(8 * t + depth, 4, stride=64), :]
            b = mask[pl.ds(8 * t + 7 - depth, 4, stride=64), :]
            f[0] = jnp.where(jnp.concatenate([a, b], axis=0) > 0, NAN, f[0])
            g = collide(f, force_rim)
            for i, k in enumerate(OUT if depth == 2 else range(19)):
                e[t, i] = g[k]
    for t in range(1, 7):
        values = rim_values(
            lambda k, s: e1[s, k], lambda k, s: e2[s, k], lambda k, s: e3[s, OUT.index(k)],
            t, force_rim, lane, row,
        )
        for i, v in enumerate(values):
            inner[t - 1, i] = v


def rim_kernel(force_ref, e1, e2, e3, inner, got1, got0, strip, outer, far, near, h1, h2, h3):
    lane, row = lanes(), rows()
    force_rim = rim_force(force_of(force_ref), row)
    even_z = lax.rem(lax.axis_index("gz"), 2) == 0
    even_y = lax.rem(lax.axis_index("gy"), 2) == 0
    for tile in range(5):
        a, b = got0[tile], got1[tile]
        take_a = even_z == ((lane & 7) < 4)
        both = jnp.where(take_a, a, b)
        for s in range(16):
            i = tile * 16 + s
            if i >= 76:
                break
            k, p = i // 4, i % 4
            strip[k, 8 * p : 8 * p + 8, :] = pltpu.roll(both, 128 - 8 * s, axis=1) if s else both
    for depth, h in enumerate((h1, h2, h3)):
        f = [edges(strip.at[k], strip.at[FLIP[k]], depth, 7 - depth) for k in range(19)]
        g = collide(f, force_rim)
        for i, k in enumerate(OUT if depth == 2 else range(19)):
            h[i] = g[k]

    def halves(v):
        w = jnp.where(even_y, pltpu.roll(v, 4, axis=0), v)
        return w[4:8], w[0:4]

    packed = [jnp.zeros((8, 128), F32)] * 2
    for t in (8, 0, 7):
        values = rim_values(
            lambda k, s: h1[k] if s == 8 else e1[s, k],
            lambda k, s: h2[k] if s == 8 else e2[s, k],
            lambda k, s: h3[OUT.index(k)] if s == 8 else e3[s, OUT.index(k)],
            t, force_rim, lane, row,
        )
        for i, v in enumerate(values):
            if i < 19:
                outer[(0, 7, 8).index(t), i] = v
            if t == 8:
                tile, s = divmod(i, 16)
                packed[tile] = jnp.where(lane // 8 == s, pltpu.roll(v, (8 * s + 4) % 128, axis=1), packed[tile])
            else:
                far[8 * i + t], near[8 * i + t] = halves(v)
    for tile in range(2):
        far[192 + tile], near[192 + tile] = halves(packed[tile])
    for t in range(1, 7):
        for i in range(NMSG):
            far[8 * i + t], near[8 * i + t] = halves(inner[t - 1, i])


def middle_kernel(force_ref, pop, mask, strip, r2, r1):
    lane = lanes()
    force = force_of(force_ref)

    @pl.loop(0, 8, unroll=2)
    def _(t):
        for p in range(4):
            at = pl.ds(pl.multiple_of(64 * p + 8 * t, 8), 8)
            f = [pop[k, at, :] for k in range(19)]
            f[0] = jnp.where(mask[at, :] > 0, NAN, f[0])
            g = collide(f, force)
            for k in range(19):
                r1[t, k, 8 * p : 8 * p + 8, :] = g[k]

    for p in range(4):
        g = collide([strip[k, 8 * p : 8 * p + 8, :] for k in range(19)], force)
        for k in range(19):
            r1[8, k, 8 * p : 8 * p + 8, :] = g[k]

    def load(k, s, p, cy):
        v = r1[s, k, 8 * p : 8 * p + 8, :]
        return pltpu.roll(v, cy % 8, axis=0) if cy else v

    @pl.loop(0, 9, unroll=3)
    def _(t):
        for p in range(4):
            g = collide(stream_own(load, p, t, lane), force)
            for k in range(19):
                r2[t, k, 8 * p : 8 * p + 8, :] = g[k]


def last_kernel(
    force_ref, r2_in, inner, outer, far, near, mask, density, velocity, r2, r3, got, got2, r2h, r2e
):
    def load2(k, s, p, cy):
        return r2[s, k, pl.ds(10 * p + 1 - cy, 8), :]

    def load3(k, s, p, cy):
        return r3[s, k, pl.ds(10 * p + 1 - cy, 8), :]

    def around(ref, t, k, v):
        ref[t, k, pl.ds(0, 4, stride=10), :] = v[0:4]
        ref[t, FLIP[k], pl.ds(9, 4, stride=10), :] = v[4:8]

    lane, row = lanes(), rows()
    force = force_of(force_ref)
    force_rim = rim_force(force, row)
    even_y = lax.rem(lax.axis_index("gy"), 2) == 0

    def halves(at):
        v = jnp.concatenate([near[at], far[at]], axis=0)
        return jnp.where(even_y, pltpu.roll(v, 4, axis=0), v)

    packed = [halves(192), halves(193)]

    def received(i, t):
        if t < 8:
            return halves(8 * i + t)
        tile, s = divmod(i, 16)
        return pltpu.roll(packed[tile], (124 - 8 * s) % 128, axis=1)

    def edge(i, t):
        return outer[(0, 7, 8).index(t), i] if t in (0, 7, 8) else inner[t - 1, i]

    for t in range(9):
        for i in range(5):
            got[i, t] = received(i, t)

    for t in range(9):
        for k in range(19):
            for p in range(4):
                r2[t, k, pl.ds(10 * p + 1, 8), :] = r2_in[t, k, 8 * p : 8 * p + 8, :]
        f = [None] * 19
        for i, k in enumerate(LOCAL):
            f[k] = edge(5 + i, t)
        for i, k in enumerate(IN):
            own = edge(OUT.index(OPP[k]), t)
            f[k] = stream_rim(lambda s, i=i: got[i, s], own, k, t, lane, row)
        g = collide(f, force_rim)
        for k in range(19):
            r2[t, k, pl.ds(1, 4, stride=10), :] = g[k][0:4]
            r2[t, FLIP[k], pl.ds(8, 4, stride=10), :] = g[k][4:8]
        for i, k in enumerate(OUT):
            r2e[i, t] = g[k]
        f = [None] * 19
        for i, k in enumerate(LOCAL):
            f[FLIP[k]] = received(5 + i, t)
        for i, k in enumerate(OUT):
            own = got[IN.index(OPP[k]), t]
            f[k] = stream_rim(lambda s, i=i: edge(i, s), own, k, t, lane, row)
        g = collide(f, force_rim)
        for i, k in enumerate(IN + FLAT + OUT):
            r2h[i, t] = g[k]
            if k in IN:
                around(r2, t, k, g[k])
        for i in range(5):
            got2[i, t] = received(19 + i, t)

    place = {k: i for i, k in enumerate(IN + FLAT + OUT)}

    for t in range(9):
        f = [None] * 19
        for k in range(19):
            own = r2h[place[OPP[k]], t]
            if k == 0:
                f[k] = own
            elif k in FLAT:
                f[k] = stream_rim(lambda s, k=k: r2h[place[k], s], own, k, t, lane, row)
            elif k in IN:
                f[k] = stream_rim(lambda s, k=k: got2[IN.index(k), s], own, k, t, lane, row)
            else:
                f[k] = stream_rim(lambda s, k=k: r2e[OUT.index(k), s], own, k, t, lane, row)
        g = collide(f, force_rim)
        for k in IN:
            around(r3, t, k, g[k])
        for p in range(4):
            g = collide(stream_own(load2, p, t, lane), force)
            for k in range(19):
                r3[t, k, pl.ds(10 * p + 1, 8), :] = g[k]

    for t in range(8):
        at = pl.ds(t * 128, 128)
        for p in range(4):
            f = stream_own(load3, p, t, lane)
            rho = f[0]
            for k in range(1, 19):
                rho = rho + f[k]
            solid = mask[p, :, at] > 0
            density[p, :, at] = jnp.where(solid, 0.0, rho)
            inv = (1.0 / MACH) / rho
            for a in range(3):
                plus = [f[k] for k in range(19) if VEL[k][a] == 1]
                minus = [f[k] for k in range(19) if VEL[k][a] == -1]
                j = plus[0] - minus[0]
                for x, y in zip(plus[1:], minus[1:]):
                    j = j + (x - y)
                velocity[a, p, :, at] = jnp.where(solid, 0.0, j * inv)


VMEM = pl.BlockSpec(memory_space=pltpu.VMEM)
HBM = pl.BlockSpec(memory_space=pltpu.HBM)


def call(kernel, name, us, out_shape, in_specs, out_specs, scratch, room=40):
    return pl.pallas_call(
        kernel,
        out_shape=out_shape,
        in_specs=in_specs,
        out_specs=out_specs,
        scratch_shapes=scratch,
        compiler_params=pltpu.CompilerParams(vmem_limit_bytes=room * 1024 * 1024),
        cost_estimate=pl.CostEstimate(
            flops=int(us * 1e6), bytes_accessed=int(us * 3e6), transcendentals=0
        ),
        name=name,
    )


def sds(*shape):
    return jax.ShapeDtypeStruct(shape, F32)


def buf(*shape):
    return pltpu.VMEM(shape, F32)


def swap(x, axis, parity):
    count = lax.axis_size(axis)
    pairs = [(i, (i + 1) % count if i % 2 == parity else (i - 1) % count) for i in range(count)]
    return lax.ppermute(x, axis, pairs)


def tiles(x):
    lead = x.shape[:-3]
    planes, height, width = x.shape[-3:]
    x = x.reshape(lead + (planes, height, width // 128, 128))
    x = jnp.swapaxes(x, -3, -2)
    return x.reshape(lead + (planes * height * width // 128, 128))


def local(pop, mask, force):
    far_memory = [pltpu.with_memory_space_constraint(x, pltpu.HBM) for x in (pop, mask, force)]
    z1, z0, mask, force = call(
        pack_kernel, "pack", 0.7,
        (sds(5, 8, 128), sds(5, 8, 128), jax.ShapeDtypeStruct(mask.shape, mask.dtype), sds(3, 8, 128)),
        [HBM] * 3, (VMEM,) * 4,
        [buf(19, 4, 8, 128), buf(19, 4, 8, 128), pltpu.SMEM((3,), F32),
         pltpu.SemaphoreType.DMA((2 + 2 * len(GROUPS),))],
    )(*far_memory)
    got1 = swap(z1, "gz", 1)
    got0 = swap(z0, "gz", 0)
    pop_tiles, mask_tiles = tiles(pop), tiles(mask)
    e1, e2, e3, inner = call(
        edge_kernel, "edge", 2.0,
        (sds(8, 19, 8, 128), sds(8, 19, 8, 128), sds(8, 5, 8, 128), sds(6, NMSG, 8, 128)),
        [VMEM] * 3, (VMEM,) * 4, [],
    )(force, pop_tiles, mask_tiles)
    strip, outer, far, near = call(
        rim_kernel, "rim", 1.0,
        (sds(19, 32, 128), sds(3, 19, 8, 128), sds(194, 4, 128), sds(194, 4, 128)),
        [VMEM] * 7, (VMEM,) * 4,
        [buf(19, 8, 128), buf(19, 8, 128), buf(5, 8, 128)],
    )(force, e1, e2, e3, inner, got1, got0)
    far = swap(far, "gy", 1)
    near = swap(near, "gy", 0)
    r2 = call(
        middle_kernel, "middle", 3.0,
        sds(9, 19, 32, 128), [VMEM] * 4, VMEM, [buf(9, 19, 32, 128)],
    )(force, pop_tiles, mask_tiles, strip)
    return call(
        last_kernel, "last", 4.0,
        (sds(4, 8, 1024), sds(3, 4, 8, 1024)),
        [VMEM] * 7, (VMEM, VMEM),
        [buf(9, 19, 40, 128), buf(9, 19, 40, 128), buf(5, 9, 8, 128), buf(5, 9, 8, 128),
         buf(19, 9, 8, 128), buf(5, 9, 8, 128)],
    )(force, r2, inner, outer, far, near, mask)


def solution(mesh):
    return jax.shard_map(
        local,
        mesh=mesh,
        in_specs=(P(None, None, "gy", "gz"), P(None, "gy", "gz"), P()),
        out_specs=(P(None, "gy", "gz"), P(None, None, "gy", "gz")),
        check_vma=False,
    )
```

```python
import jax
import jax.numpy as jnp
from jax import lax
from jax.experimental import pallas as pl
from jax.experimental.pallas import tpu as pltpu
from jax.sharding import PartitionSpec as P

VEL = [
    (0, 0, 0),
    (1, 0, 0),
    (-1, 0, 0),
    (0, 1, 0),
    (0, -1, 0),
    (0, 0, 1),
    (0, 0, -1),
    (1, 1, 0),
    (-1, -1, 0),
    (1, -1, 0),
    (-1, 1, 0),
    (1, 0, 1),
    (-1, 0, -1),
    (1, 0, -1),
    (-1, 0, 1),
    (0, 1, 1),
    (0, -1, -1),
    (0, 1, -1),
    (0, -1, 1),
]
OPP = [VEL.index((-x, -y, -z)) for x, y, z in VEL]
FLIP = [VEL.index((x, -y, z)) for x, y, z in VEL]
IN = [k for k in range(19) if VEL[k][1] == 1]
OUT = [FLIP[k] for k in IN]
FLAT = [k for k in range(19) if VEL[k][1] == 0]
LOCAL = FLAT + OUT
NMSG = 24
MACH = 0.05
BIG = 1e30
NAN = float("nan")
F32 = jnp.float32


def lanes():
    return lax.broadcasted_iota(jnp.int32, (8, 128), 1)


def rows():
    return lax.broadcasted_iota(jnp.int32, (8, 128), 0)


def collide(f, force):
    fx, fy, fz = force
    sx, dx = f[1] + f[2], f[1] - f[2]
    sy, dy = f[3] + f[4], f[3] - f[4]
    sz, dz = f[5] + f[6], f[5] - f[6]

    def plane(a):
        big, small = f[a] + f[a + 1], f[a] - f[a + 1]
        big2, small2 = f[a + 2] + f[a + 3], f[a + 2] - f[a + 3]
        return big + big2, big - big2, small + small2, small - small2, (small, small2)

    nxy, mxy, tyyx, txxy, odd_xy = plane(7)
    nxz, mxz, tzzx, txxz, odd_xz = plane(11)
    nyz, myz, tzzy, tyyz, odd_yz = plane(15)
    tx, ty, tz = tyyx + tzzx, txxy + tzzy, txxz + tyyz
    jx, jy, jz = dx + tx, dy + ty, dz + tz
    nx, ny, nz = nxy + nxz, nxy + nyz, nxz + nyz
    total_s = (sx + sy) + sz
    total_n = nx + nyz
    rho = (f[0] + total_s) + total_n
    inv = 0.3125 / rho
    vx, vy, vz = jx * inv, jy * inv, jz * inv
    gx, gy, gz = jx * vx, jy * vy, jz * vz
    total_g = (gx + gy) + gz
    mxy = jx * vy - 0.0625 * mxy
    mxz = jx * vz - 0.0625 * mxz
    myz = jy * vz - 0.0625 * myz
    base = rho * (1.3 / 36.0) + total_g * (1.3 / 3.75)
    nxy = (base - 0.52 * gz) - 0.075 * nxy
    nxz = (base - 0.52 * gy) - 0.075 * nxz
    nyz = (base - 0.52 * gx) - 0.075 * nyz
    bx = jx * (0.4 / 3.0) + fx * (1.0 / 12.0)
    by = jy * (0.4 / 3.0) + fy * (1.0 / 12.0)
    bz = jz * (0.4 / 3.0) + fz * (1.0 / 12.0)
    rest = rho * (1.25 / 6.0 - 5.2 / 36.0) + total_g * (1.04 - 5.2 / 3.75)
    out = [None] * 19

    def axis(a, g, s, n, d, t, force_a):
        even = ((rest + 0.96 * g) - 0.125 * s) + 0.025 * n
        odd = (0.8 / 3.0 * t - 0.1 / 3.0 * d) + force_a * (1.0 / 6.0)
        out[a], out[a + 1] = even + odd, even - odd

    def edge(a, n, m, b1, b2, p, q):
        big, big2 = n + m, n - m
        small, small2 = (b1 + b2) - 0.3 * p, (b1 - b2) - 0.3 * q
        out[a], out[a + 1] = big + small, big - small
        out[a + 2], out[a + 3] = big2 + small2, big2 - small2

    axis(1, gx, sx, nx, dx, tx, fx)
    axis(3, gy, sy, ny, dy, ty, fy)
    axis(5, gz, sz, nz, dz, tz, fz)
    edge(7, nxy, mxy, bx, by, *odd_xy)
    edge(11, nxz, mxz, bx, bz, *odd_xz)
    edge(15, nyz, myz, by, bz, *odd_yz)
    out[0] = (rho * (1.0 - 1.25 + 15.6 / 36.0) + total_g * (15.6 / 3.75 - 6.08)) + (
        0.25 * total_s + 0.2 * total_n
    )
    return out


def along_z(get, t, cz, lane):
    cur = get(t)
    if cz == 0:
        return cur
    if cz == 1:
        before = get((t + 8) % 9 if isinstance(t, int) else jnp.where(t == 0, 8, t - 1))
        return pltpu.roll(jnp.where(lane == 127, before, cur), 1, axis=1)
    after = get((t + 1) % 9 if isinstance(t, int) else jnp.where(t == 8, 0, t + 1))
    return pltpu.roll(jnp.where(lane == 0, after, cur), 127, axis=1)


def stream_own(load, p, t, lane):
    f = []
    for k in range(19):
        cx, cy, cz = VEL[k]
        own = load(OPP[k], t, p, 0)
        q = p - cx
        if k == 0 or q < 0 or q > 3:
            f.append(own)
            continue
        v = along_z(lambda s, k=k, q=q, cy=cy: load(k, s, q, cy), t, cz, lane)
        f.append(jnp.where(v < BIG, v, own))
    return f


def stream_rim(get, own, k, t, lane, row):
    cx, _, cz = VEL[k]
    v = along_z(get, t, cz, lane)
    if cx:
        v = pltpu.roll(v, cx % 8, axis=0)
        wall = (row & 3) == (0 if cx == 1 else 3)
        v = jnp.where(wall, NAN, v)
    return jnp.where(v < BIG, v, own)


def edges(ref, flipped, lower, upper):
    a = ref[pl.ds(lower, 4, stride=8), :]
    b = flipped[pl.ds(upper, 4, stride=8), :]
    return jnp.concatenate([a, b], axis=0)


def force_of(force_ref):
    return force_ref[0], force_ref[1], force_ref[2]


def rim_force(force, row):
    fx, fy, fz = force
    return fx, jnp.where(row < 4, fy, -fy), fz


GROUPS = ((0, 10), (10, 19))


def pack_kernel(pop_hbm, mask_hbm, force_hbm, out1, out0, mask, force, first, last, given, sem):
    copies = [
        pltpu.make_async_copy(mask_hbm, mask, sem.at[0]),
        pltpu.make_async_copy(force_hbm, given, sem.at[1]),
    ]
    for i, (a, b) in enumerate(GROUPS):
        for j, (at, to) in enumerate(((0, first), (896, last))):
            copies.append(
                pltpu.make_async_copy(
                    pop_hbm.at[a:b, :, :, at : at + 128], to.at[a:b], sem.at[2 + 2 * i + j]
                )
            )
    for copy in copies:
        copy.start()
    copies[0].wait()
    copies[1].wait()
    for i in range(3):
        force[i] = jnp.full((8, 128), given[i], F32)
    lane = lanes()
    even = lax.rem(lax.axis_index("gz"), 2) == 0
    group = lane // 8
    left = [jnp.zeros((8, 128), F32)] * 5
    right = [jnp.zeros((8, 128), F32)] * 5
    for n, (k0, k1) in enumerate(GROUPS):
        copies[2 + 2 * n].wait()
        copies[3 + 2 * n].wait()
        for k in range(k0, k1):
            for p in range(4):
                tile, s = divmod(4 * k + p, 16)
                a, b = first[k, p], last[k, p]
                if k == 0:
                    a = jnp.where(mask[p, :, 0:128] > 0, NAN, a)
                    b = jnp.where(mask[p, :, 896:1024] > 0, NAN, b)
                if s:
                    a = pltpu.roll(a, 8 * s, axis=1)
                    b = pltpu.roll(b, 8 * s, axis=1)
                left[tile] = jnp.where(group == s, a, left[tile])
                right[tile] = jnp.where(group == (s + 15) % 16, b, right[tile])
    for tile in range(5):
        out0[tile] = jnp.where(even, right[tile], left[tile])
        out1[tile] = jnp.where(even, left[tile], right[tile])


def rim_values(e1, e2, e3, t, force_rim, lane, row):
    own = [e1(k, t) for k in range(19)]
    values = [own[k] for k in OUT]
    for k in LOCAL:
        if k == 0:
            values.append(own[0])
        else:
            src = e1 if k in FLAT else e2
            values.append(stream_rim(lambda s, k=k, src=src: src(k, s), own[OPP[k]], k, t, lane, row))
    own = [e2(k, t) for k in range(19)]
    f = [own[0]]
    for k in range(1, 19):
        src = e2 if k in FLAT else (e1 if k in IN else e3)
        f.append(stream_rim(lambda s, k=k, src=src: src(k, s), own[OPP[k]], k, t, lane, row))
    g = collide(f, force_rim)
    return values + [g[k] for k in OUT]


def edge_kernel(force_ref, pop, mask, e1, e2, e3, inner):
    lane, row = lanes(), rows()
    force = force_of(force_ref)
    force_rim = rim_force(force, row)
    mirrored = (force[0], -force[1], force[2])
    for depth, e in enumerate((e1, e2, e3)):
        for side in range(2):
            for p in range(4):
                at = pl.ds(64 * p + (7 - depth if side else depth), 8, stride=8)
                f = [pop[FLIP[k] if side else k, at, :] for k in range(19)]
                f[0] = jnp.where(mask[at, :] > 0, NAN, f[0])
                g = collide(f, mirrored if side else force)
                for i, k in enumerate(OUT if depth == 2 else range(19)):
                    e[i, pl.ds(4 * side + p, 8, stride=8), :] = g[k]

    def tile(e):
        return lambda k, t: e[OUT.index(k) if e is e3 else k, 8 * t : 8 * t + 8, :]

    for t in range(1, 7):
        values = rim_values(tile(e1), tile(e2), tile(e3), t, force_rim, lane, row)
        for i, v in enumerate(values):
            inner[t - 1, i] = v


def rim_kernel(force_ref, e1, e2, e3, inner, got1, got0, strip, outer, far, near, h1, h2, h3):
    lane, row = lanes(), rows()
    force_rim = rim_force(force_of(force_ref), row)
    even_z = lax.rem(lax.axis_index("gz"), 2) == 0
    even_y = lax.rem(lax.axis_index("gy"), 2) == 0
    for tile in range(5):
        a, b = got0[tile], got1[tile]
        take_a = even_z == ((lane & 7) < 4)
        both = jnp.where(take_a, a, b)
        for s in range(16):
            i = tile * 16 + s
            if i >= 76:
                break
            k, p = i // 4, i % 4
            strip[k, 8 * p : 8 * p + 8, :] = pltpu.roll(both, 128 - 8 * s, axis=1) if s else both
    for depth, h in enumerate((h1, h2, h3)):
        f = [edges(strip.at[k], strip.at[FLIP[k]], depth, 7 - depth) for k in range(19)]
        g = collide(f, force_rim)
        for i, k in enumerate(OUT if depth == 2 else range(19)):
            h[i] = g[k]

    def halves(v):
        w = jnp.where(even_y, pltpu.roll(v, 4, axis=0), v)
        return w[4:8], w[0:4]

    packed = [jnp.zeros((8, 128), F32)] * 2
    for t in (8, 0, 7):
        values = rim_values(
            lambda k, s: h1[k] if s == 8 else e1[k, 8 * s : 8 * s + 8, :],
            lambda k, s: h2[k] if s == 8 else e2[k, 8 * s : 8 * s + 8, :],
            lambda k, s: h3[OUT.index(k)] if s == 8 else e3[OUT.index(k), 8 * s : 8 * s + 8, :],
            t, force_rim, lane, row,
        )
        for i, v in enumerate(values):
            if i < 19:
                outer[(0, 7, 8).index(t), i] = v
            if t == 8:
                tile, s = divmod(i, 16)
                packed[tile] = jnp.where(lane // 8 == s, pltpu.roll(v, (8 * s + 4) % 128, axis=1), packed[tile])
            else:
                far[8 * i + t], near[8 * i + t] = halves(v)
    for tile in range(2):
        far[192 + tile], near[192 + tile] = halves(packed[tile])
    for t in range(1, 7):
        for i in range(NMSG):
            far[8 * i + t], near[8 * i + t] = halves(inner[t - 1, i])


def middle_kernel(force_ref, pop, mask, strip, r2, r1):
    lane = lanes()
    force = force_of(force_ref)

    @pl.loop(0, 8, unroll=2)
    def _(t):
        for p in range(4):
            at = pl.ds(pl.multiple_of(64 * p + 8 * t, 8), 8)
            f = [pop[k, at, :] for k in range(19)]
            f[0] = jnp.where(mask[at, :] > 0, NAN, f[0])
            g = collide(f, force)
            for k in range(19):
                r1[t, k, 8 * p : 8 * p + 8, :] = g[k]

    for p in range(4):
        g = collide([strip[k, 8 * p : 8 * p + 8, :] for k in range(19)], force)
        for k in range(19):
            r1[8, k, 8 * p : 8 * p + 8, :] = g[k]

    def load(k, s, p, cy):
        v = r1[s, k, 8 * p : 8 * p + 8, :]
        return pltpu.roll(v, cy % 8, axis=0) if cy else v

    @pl.loop(0, 9, unroll=3)
    def _(t):
        for p in range(4):
            g = collide(stream_own(load, p, t, lane), force)
            for k in range(19):
                r2[t, k, 8 * p : 8 * p + 8, :] = g[k]


def last_kernel(
    force_ref, r2_in, inner, outer, far, near, mask, density, velocity, r2, r3, got, got2, r2h, r2e
):
    def load2(k, s, p, cy):
        return r2[s, k, pl.ds(10 * p + 1 - cy, 8), :]

    def load3(k, s, p, cy):
        return r3[s, k, pl.ds(10 * p + 1 - cy, 8), :]

    def around(ref, t, k, v):
        ref[t, k, pl.ds(0, 4, stride=10), :] = v[0:4]
        ref[t, FLIP[k], pl.ds(9, 4, stride=10), :] = v[4:8]

    lane, row = lanes(), rows()
    force = force_of(force_ref)
    force_rim = rim_force(force, row)
    even_y = lax.rem(lax.axis_index("gy"), 2) == 0

    def halves(at):
        v = jnp.concatenate([near[at], far[at]], axis=0)
        return jnp.where(even_y, pltpu.roll(v, 4, axis=0), v)

    packed = [halves(192), halves(193)]

    def received(i, t):
        if t < 8:
            return halves(8 * i + t)
        tile, s = divmod(i, 16)
        return pltpu.roll(packed[tile], (124 - 8 * s) % 128, axis=1)

    def edge(i, t):
        return outer[(0, 7, 8).index(t), i] if t in (0, 7, 8) else inner[t - 1, i]

    for t in range(9):
        for i in range(5):
            got[i, t] = received(i, t)

    for t in range(9):
        for k in range(19):
            for p in range(4):
                r2[t, k, pl.ds(10 * p + 1, 8), :] = r2_in[t, k, 8 * p : 8 * p + 8, :]
        f = [None] * 19
        for i, k in enumerate(LOCAL):
            f[k] = edge(5 + i, t)
        for i, k in enumerate(IN):
            own = edge(OUT.index(OPP[k]), t)
            f[k] = stream_rim(lambda s, i=i: got[i, s], own, k, t, lane, row)
        g = collide(f, force_rim)
        for k in range(19):
            r2[t, k, pl.ds(1, 4, stride=10), :] = g[k][0:4]
            r2[t, FLIP[k], pl.ds(8, 4, stride=10), :] = g[k][4:8]
        for i, k in enumerate(OUT):
            r2e[i, t] = g[k]
        f = [None] * 19
        for i, k in enumerate(LOCAL):
            f[FLIP[k]] = received(5 + i, t)
        for i, k in enumerate(OUT):
            own = got[IN.index(OPP[k]), t]
            f[k] = stream_rim(lambda s, i=i: edge(i, s), own, k, t, lane, row)
        g = collide(f, force_rim)
        for i, k in enumerate(IN + FLAT + OUT):
            r2h[i, t] = g[k]
            if k in IN:
                around(r2, t, k, g[k])
        for i in range(5):
            got2[i, t] = received(19 + i, t)

    place = {k: i for i, k in enumerate(IN + FLAT + OUT)}

    for t in range(9):
        f = [None] * 19
        for k in range(19):
            own = r2h[place[OPP[k]], t]
            if k == 0:
                f[k] = own
            elif k in FLAT:
                f[k] = stream_rim(lambda s, k=k: r2h[place[k], s], own, k, t, lane, row)
            elif k in IN:
                f[k] = stream_rim(lambda s, k=k: got2[IN.index(k), s], own, k, t, lane, row)
            else:
                f[k] = stream_rim(lambda s, k=k: r2e[OUT.index(k), s], own, k, t, lane, row)
        g = collide(f, force_rim)
        for k in IN:
            around(r3, t, k, g[k])
        for p in range(4):
            g = collide(stream_own(load2, p, t, lane), force)
            for k in range(19):
                r3[t, k, pl.ds(10 * p + 1, 8), :] = g[k]

    for t in range(8):
        at = pl.ds(t * 128, 128)
        for p in range(4):
            f = stream_own(load3, p, t, lane)
            rho = f[0]
            for k in range(1, 19):
                rho = rho + f[k]
            solid = mask[p, :, at] > 0
            density[p, :, at] = jnp.where(solid, 0.0, rho)
            inv = (1.0 / MACH) / rho
            for a in range(3):
                plus = [f[k] for k in range(19) if VEL[k][a] == 1]
                minus = [f[k] for k in range(19) if VEL[k][a] == -1]
                j = plus[0] - minus[0]
                for x, y in zip(plus[1:], minus[1:]):
                    j = j + (x - y)
                velocity[a, p, :, at] = jnp.where(solid, 0.0, j * inv)


VMEM = pl.BlockSpec(memory_space=pltpu.VMEM)
HBM = pl.BlockSpec(memory_space=pltpu.HBM)


def call(kernel, name, us, out_shape, in_specs, out_specs, scratch, room=40):
    return pl.pallas_call(
        kernel,
        out_shape=out_shape,
        in_specs=in_specs,
        out_specs=out_specs,
        scratch_shapes=scratch,
        compiler_params=pltpu.CompilerParams(vmem_limit_bytes=room * 1024 * 1024),
        cost_estimate=pl.CostEstimate(
            flops=int(us * 1e6), bytes_accessed=int(us * 3e6), transcendentals=0
        ),
        name=name,
    )


def sds(*shape):
    return jax.ShapeDtypeStruct(shape, F32)


def buf(*shape):
    return pltpu.VMEM(shape, F32)


def swap(x, axis, parity):
    count = lax.axis_size(axis)
    pairs = [(i, (i + 1) % count if i % 2 == parity else (i - 1) % count) for i in range(count)]
    return lax.ppermute(x, axis, pairs)


def tiles(x):
    lead = x.shape[:-3]
    planes, height, width = x.shape[-3:]
    x = x.reshape(lead + (planes, height, width // 128, 128))
    x = jnp.swapaxes(x, -3, -2)
    return x.reshape(lead + (planes * height * width // 128, 128))


def local(pop, mask, force):
    far_memory = [pltpu.with_memory_space_constraint(x, pltpu.HBM) for x in (pop, mask, force)]
    z1, z0, mask, force = call(
        pack_kernel, "pack", 0.7,
        (sds(5, 8, 128), sds(5, 8, 128), jax.ShapeDtypeStruct(mask.shape, mask.dtype), sds(3, 8, 128)),
        [HBM] * 3, (VMEM,) * 4,
        [buf(19, 4, 8, 128), buf(19, 4, 8, 128), pltpu.SMEM((3,), F32),
         pltpu.SemaphoreType.DMA((2 + 2 * len(GROUPS),))],
    )(*far_memory)
    got1 = swap(z1, "gz", 1)
    got0 = swap(z0, "gz", 0)
    pop_tiles, mask_tiles = tiles(pop), tiles(mask)
    e1, e2, e3, inner = call(
        edge_kernel, "edge", 2.0,
        (sds(19, 64, 128), sds(19, 64, 128), sds(5, 64, 128), sds(6, NMSG, 8, 128)),
        [VMEM] * 3, (VMEM,) * 4, [],
    )(force, pop_tiles, mask_tiles)
    strip, outer, far, near = call(
        rim_kernel, "rim", 1.0,
        (sds(19, 32, 128), sds(3, 19, 8, 128), sds(194, 4, 128), sds(194, 4, 128)),
        [VMEM] * 7, (VMEM,) * 4,
        [buf(19, 8, 128), buf(19, 8, 128), buf(5, 8, 128)],
    )(force, e1, e2, e3, inner, got1, got0)
    far = swap(far, "gy", 1)
    near = swap(near, "gy", 0)
    r2 = call(
        middle_kernel, "middle", 3.0,
        sds(9, 19, 32, 128), [VMEM] * 4, VMEM, [buf(9, 19, 32, 128)],
    )(force, pop_tiles, mask_tiles, strip)
    return call(
        last_kernel, "last", 4.0,
        (sds(4, 8, 1024), sds(3, 4, 8, 1024)),
        [VMEM] * 7, (VMEM, VMEM),
        [buf(9, 19, 40, 128), buf(9, 19, 40, 128), buf(5, 9, 8, 128), buf(5, 9, 8, 128),
         buf(19, 9, 8, 128), buf(5, 9, 8, 128)],
    )(force, r2, inner, outer, far, near, mask)


def solution(mesh):
    return jax.shard_map(
        local,
        mesh=mesh,
        in_specs=(P(None, None, "gy", "gz"), P(None, "gy", "gz"), P()),
        out_specs=(P(None, "gy", "gz"), P(None, None, "gy", "gz")),
        check_vma=False,
    )
```

```python
import jax
import jax.numpy as jnp
from jax import lax
from jax.experimental import pallas as pl
from jax.experimental.pallas import tpu as pltpu
from jax.sharding import PartitionSpec as P

VEL = [
    (0, 0, 0),
    (1, 0, 0),
    (-1, 0, 0),
    (0, 1, 0),
    (0, -1, 0),
    (0, 0, 1),
    (0, 0, -1),
    (1, 1, 0),
    (-1, -1, 0),
    (1, -1, 0),
    (-1, 1, 0),
    (1, 0, 1),
    (-1, 0, -1),
    (1, 0, -1),
    (-1, 0, 1),
    (0, 1, 1),
    (0, -1, -1),
    (0, 1, -1),
    (0, -1, 1),
]
OPP = [VEL.index((-x, -y, -z)) for x, y, z in VEL]
FLIP = [VEL.index((x, -y, z)) for x, y, z in VEL]
IN = [k for k in range(19) if VEL[k][1] == 1]
OUT = [FLIP[k] for k in IN]
FLAT = [k for k in range(19) if VEL[k][1] == 0]
LOCAL = FLAT + OUT
NMSG = 24
MACH = 0.05
BIG = 1e30
NAN = float("nan")
F32 = jnp.float32


def lanes():
    return lax.broadcasted_iota(jnp.int32, (8, 128), 1)


def rows():
    return lax.broadcasted_iota(jnp.int32, (8, 128), 0)


def collide(f, force):
    fx, fy, fz = force
    sx, dx = f[1] + f[2], f[1] - f[2]
    sy, dy = f[3] + f[4], f[3] - f[4]
    sz, dz = f[5] + f[6], f[5] - f[6]

    def plane(a):
        big, small = f[a] + f[a + 1], f[a] - f[a + 1]
        big2, small2 = f[a + 2] + f[a + 3], f[a + 2] - f[a + 3]
        return big + big2, big - big2, small + small2, small - small2, (small, small2)

    nxy, mxy, tyyx, txxy, odd_xy = plane(7)
    nxz, mxz, tzzx, txxz, odd_xz = plane(11)
    nyz, myz, tzzy, tyyz, odd_yz = plane(15)
    tx, ty, tz = tyyx + tzzx, txxy + tzzy, txxz + tyyz
    jx, jy, jz = dx + tx, dy + ty, dz + tz
    nx, ny, nz = nxy + nxz, nxy + nyz, nxz + nyz
    total_s = (sx + sy) + sz
    total_n = nx + nyz
    rho = (f[0] + total_s) + total_n
    inv = 0.3125 / rho
    vx, vy, vz = jx * inv, jy * inv, jz * inv
    gx, gy, gz = jx * vx, jy * vy, jz * vz
    total_g = (gx + gy) + gz
    mxy = jx * vy - 0.0625 * mxy
    mxz = jx * vz - 0.0625 * mxz
    myz = jy * vz - 0.0625 * myz
    base = rho * (1.3 / 36.0) + total_g * (1.3 / 3.75)
    nxy = (base - 0.52 * gz) - 0.075 * nxy
    nxz = (base - 0.52 * gy) - 0.075 * nxz
    nyz = (base - 0.52 * gx) - 0.075 * nyz
    bx = jx * (0.4 / 3.0) + fx * (1.0 / 12.0)
    by = jy * (0.4 / 3.0) + fy * (1.0 / 12.0)
    bz = jz * (0.4 / 3.0) + fz * (1.0 / 12.0)
    rest = rho * (1.25 / 6.0 - 5.2 / 36.0) + total_g * (1.04 - 5.2 / 3.75)
    out = [None] * 19

    def axis(a, g, s, n, d, t, force_a):
        even = ((rest + 0.96 * g) - 0.125 * s) + 0.025 * n
        odd = (0.8 / 3.0 * t - 0.1 / 3.0 * d) + force_a * (1.0 / 6.0)
        out[a], out[a + 1] = even + odd, even - odd

    def edge(a, n, m, b1, b2, p, q):
        big, big2 = n + m, n - m
        small, small2 = (b1 + b2) - 0.3 * p, (b1 - b2) - 0.3 * q
        out[a], out[a + 1] = big + small, big - small
        out[a + 2], out[a + 3] = big2 + small2, big2 - small2

    axis(1, gx, sx, nx, dx, tx, fx)
    axis(3, gy, sy, ny, dy, ty, fy)
    axis(5, gz, sz, nz, dz, tz, fz)
    edge(7, nxy, mxy, bx, by, *odd_xy)
    edge(11, nxz, mxz, bx, bz, *odd_xz)
    edge(15, nyz, myz, by, bz, *odd_yz)
    out[0] = (rho * (1.0 - 1.25 + 15.6 / 36.0) + total_g * (15.6 / 3.75 - 6.08)) + (
        0.25 * total_s + 0.2 * total_n
    )
    return out


def along_z(get, t, cz, lane):
    cur = get(t)
    if cz == 0:
        return cur
    if cz == 1:
        before = get((t + 8) % 9 if isinstance(t, int) else jnp.where(t == 0, 8, t - 1))
        return pltpu.roll(jnp.where(lane == 127, before, cur), 1, axis=1)
    after = get((t + 1) % 9 if isinstance(t, int) else jnp.where(t == 8, 0, t + 1))
    return pltpu.roll(jnp.where(lane == 0, after, cur), 127, axis=1)


def stream_own(load, p, t, lane):
    f = []
    for k in range(19):
        cx, cy, cz = VEL[k]
        own = load(OPP[k], t, p, 0)
        q = p - cx
        if k == 0 or q < 0 or q > 3:
            f.append(own)
            continue
        v = along_z(lambda s, k=k, q=q, cy=cy: load(k, s, q, cy), t, cz, lane)
        f.append(jnp.where(v < BIG, v, own))
    return f


def stream_rim(get, own, k, t, lane, row):
    cx, _, cz = VEL[k]
    v = along_z(get, t, cz, lane)
    if cx:
        v = pltpu.roll(v, cx % 8, axis=0)
        wall = (row & 3) == (0 if cx == 1 else 3)
        v = jnp.where(wall, NAN, v)
    return jnp.where(v < BIG, v, own)


def edges(ref, flipped, lower, upper):
    a = ref[pl.ds(lower, 4, stride=8), :]
    b = flipped[pl.ds(upper, 4, stride=8), :]
    return jnp.concatenate([a, b], axis=0)


def force_of(force_ref):
    return force_ref[0], force_ref[1], force_ref[2]


def rim_force(force, row):
    fx, fy, fz = force
    return fx, jnp.where(row < 4, fy, -fy), fz


GROUPS = ((0, 10), (10, 19))


def pack_kernel(pop_hbm, mask_hbm, force_hbm, out1, out0, mask, force, first, last, given, sem):
    copies = [
        pltpu.make_async_copy(mask_hbm, mask, sem.at[0]),
        pltpu.make_async_copy(force_hbm, given, sem.at[1]),
    ]
    for i, (a, b) in enumerate(GROUPS):
        for j, (at, to) in enumerate(((0, first), (896, last))):
            copies.append(
                pltpu.make_async_copy(
                    pop_hbm.at[a:b, :, :, at : at + 128], to.at[a:b], sem.at[2 + 2 * i + j]
                )
            )
    for copy in copies:
        copy.start()
    copies[0].wait()
    copies[1].wait()
    for i in range(3):
        force[i] = jnp.full((8, 128), given[i], F32)
    lane = lanes()
    even = lax.rem(lax.axis_index("gz"), 2) == 0
    group = lane // 8
    left = [jnp.zeros((8, 128), F32)] * 5
    right = [jnp.zeros((8, 128), F32)] * 5
    for n, (k0, k1) in enumerate(GROUPS):
        copies[2 + 2 * n].wait()
        copies[3 + 2 * n].wait()
        for k in range(k0, k1):
            for p in range(4):
                tile, s = divmod(4 * k + p, 16)
                a, b = first[k, p], last[k, p]
                if k == 0:
                    a = jnp.where(mask[p, :, 0:128] > 0, NAN, a)
                    b = jnp.where(mask[p, :, 896:1024] > 0, NAN, b)
                if s:
                    a = pltpu.roll(a, 8 * s, axis=1)
                    b = pltpu.roll(b, 8 * s, axis=1)
                left[tile] = jnp.where(group == s, a, left[tile])
                right[tile] = jnp.where(group == (s + 15) % 16, b, right[tile])
    for tile in range(5):
        out0[tile] = jnp.where(even, right[tile], left[tile])
        out1[tile] = jnp.where(even, left[tile], right[tile])


def rim_values(e1, e2, e3, t, force_rim, lane, row):
    own = [e1(k, t) for k in range(19)]
    values = [own[k] for k in OUT]
    for k in LOCAL:
        if k == 0:
            values.append(own[0])
        else:
            src = e1 if k in FLAT else e2
            values.append(stream_rim(lambda s, k=k, src=src: src(k, s), own[OPP[k]], k, t, lane, row))
    own = [e2(k, t) for k in range(19)]
    f = [own[0]]
    for k in range(1, 19):
        src = e2 if k in FLAT else (e1 if k in IN else e3)
        f.append(stream_rim(lambda s, k=k, src=src: src(k, s), own[OPP[k]], k, t, lane, row))
    g = collide(f, force_rim)
    return values + [g[k] for k in OUT]


OWN = 4


def relax_own(t, force, pop, mask, r1):
    for p in range(4):
        at = pl.ds(64 * p + 8 * t, 8)
        f = [pop[k, at, :] for k in range(19)]
        f[0] = jnp.where(mask[at, :] > 0, NAN, f[0])
        g = collide(f, force)
        for k in range(19):
            r1[t - (OWN if t >= OWN else 0), k, 8 * p : 8 * p + 8, :] = g[k]


def edge_kernel(force_ref, pop, mask, e1, e2, e3, inner, r1):
    lane, row = lanes(), rows()
    force = force_of(force_ref)
    force_rim = rim_force(force, row)
    mirrored = (force[0], -force[1], force[2])
    for depth, e in enumerate((e1, e2, e3)):
        for side in range(2):
            for p in range(4):
                at = pl.ds(64 * p + (7 - depth if side else depth), 8, stride=8)
                f = [pop[FLIP[k] if side else k, at, :] for k in range(19)]
                f[0] = jnp.where(mask[at, :] > 0, NAN, f[0])
                g = collide(f, mirrored if side else force)
                for i, k in enumerate(OUT if depth == 2 else range(19)):
                    e[i, pl.ds(4 * side + p, 8, stride=8), :] = g[k]

    def tile(e):
        return lambda k, t: e[OUT.index(k) if e is e3 else k, 8 * t : 8 * t + 8, :]

    for t in range(1, 7):
        values = rim_values(tile(e1), tile(e2), tile(e3), t, force_rim, lane, row)
        for i, v in enumerate(values):
            inner[t - 1, i] = v
    for t in range(OWN):
        relax_own(t, force, pop, mask, r1)


def rim_kernel(force_ref, e1, e2, e3, inner, got1, got0, strip, outer, far, near, h1, h2, h3):
    lane, row = lanes(), rows()
    force_rim = rim_force(force_of(force_ref), row)
    even_z = lax.rem(lax.axis_index("gz"), 2) == 0
    even_y = lax.rem(lax.axis_index("gy"), 2) == 0
    for tile in range(5):
        a, b = got0[tile], got1[tile]
        take_a = even_z == ((lane & 7) < 4)
        both = jnp.where(take_a, a, b)
        for s in range(16):
            i = tile * 16 + s
            if i >= 76:
                break
            k, p = i // 4, i % 4
            strip[k, 8 * p : 8 * p + 8, :] = pltpu.roll(both, 128 - 8 * s, axis=1) if s else both
    for depth, h in enumerate((h1, h2, h3)):
        f = [edges(strip.at[k], strip.at[FLIP[k]], depth, 7 - depth) for k in range(19)]
        g = collide(f, force_rim)
        for i, k in enumerate(OUT if depth == 2 else range(19)):
            h[i] = g[k]

    def halves(v):
        w = jnp.where(even_y, pltpu.roll(v, 4, axis=0), v)
        return w[4:8], w[0:4]

    packed = [jnp.zeros((8, 128), F32)] * 2
    for t in (8, 0, 7):
        values = rim_values(
            lambda k, s: h1[k] if s == 8 else e1[k, 8 * s : 8 * s + 8, :],
            lambda k, s: h2[k] if s == 8 else e2[k, 8 * s : 8 * s + 8, :],
            lambda k, s: h3[OUT.index(k)] if s == 8 else e3[OUT.index(k), 8 * s : 8 * s + 8, :],
            t, force_rim, lane, row,
        )
        for i, v in enumerate(values):
            if i < 19:
                outer[(0, 7, 8).index(t), i] = v
            if t == 8:
                tile, s = divmod(i, 16)
                packed[tile] = jnp.where(lane // 8 == s, pltpu.roll(v, (8 * s + 4) % 128, axis=1), packed[tile])
            else:
                far[8 * i + t], near[8 * i + t] = halves(v)
    for tile in range(2):
        far[192 + tile], near[192 + tile] = halves(packed[tile])
    for t in range(1, 7):
        for i in range(NMSG):
            far[8 * i + t], near[8 * i + t] = halves(inner[t - 1, i])


def middle_kernel(force_ref, pop, mask, r1, strip, r3, second, third, rest, last_tile, r2):
    lane = lanes()
    force = force_of(force_ref)

    for t in range(OWN, 8):
        relax_own(t, force, pop, mask, rest)
    for p in range(4):
        g = collide([strip[k, 8 * p : 8 * p + 8, :] for k in range(19)], force)
        for k in range(19):
            last_tile[k, 8 * p : 8 * p + 8, :] = g[k]

    def load1(k, s, p, cy):
        v = (last_tile if s == 8 else r1.at[s] if s < OWN else rest.at[s - OWN])[k, 8 * p : 8 * p + 8, :]
        return pltpu.roll(v, cy % 8, axis=0) if cy else v

    def load2(k, s, p, cy):
        v = r2[s, k, 8 * p : 8 * p + 8, :]
        return pltpu.roll(v, cy % 8, axis=0) if cy else v

    for load, after in ((load1, r2), (load2, r3)):
        for t in range(9):
            for p in range(4):
                g = collide(stream_own(load, p, t, lane), force)
                for k in range(19):
                    after[t, k, 8 * p : 8 * p + 8, :] = g[k]

    for t in range(9):
        for k in range(19):
            second[k, t] = edges(r2.at[t, k], r2.at[t, FLIP[k]], 1, 6)
        for i, k in enumerate(OUT):
            third[i, t] = edges(r2.at[t, k], r2.at[t, FLIP[k]], 2, 5)


WRITE = 2


def last_kernel(
    force_ref, r3_in, second, third, inner, outer, far, near, mask, density_hbm, velocity_hbm,
    r3, got, got2, r2h, r2e, density, velocity, sem
):
    def load3(k, s, p, cy):
        return r3[s, k, pl.ds(10 * p + 1 - cy, 8), :]

    def put(t, k, v, depth):
        r3[t, k, pl.ds(depth, 4, stride=10), :] = v[0:4]
        r3[t, FLIP[k], pl.ds(9 - depth, 4, stride=10), :] = v[4:8]

    lane, row = lanes(), rows()
    force = force_of(force_ref)
    force_rim = rim_force(force, row)
    even_y = lax.rem(lax.axis_index("gy"), 2) == 0

    def halves(at):
        v = jnp.concatenate([near[at], far[at]], axis=0)
        return jnp.where(even_y, pltpu.roll(v, 4, axis=0), v)

    packed = [halves(192), halves(193)]

    def received(i, t):
        if t < 8:
            return halves(8 * i + t)
        tile, s = divmod(i, 16)
        return pltpu.roll(packed[tile], (124 - 8 * s) % 128, axis=1)

    def edge(i, t):
        return outer[(0, 7, 8).index(t), i] if t in (0, 7, 8) else inner[t - 1, i]

    for t in range(9):
        for i in range(5):
            got[i, t] = received(i, t)

    for t in range(9):
        for k in range(19):
            for p in range(4):
                r3[t, k, pl.ds(10 * p + 1, 8), :] = r3_in[t, k, 8 * p : 8 * p + 8, :]
        f = [None] * 19
        for i, k in enumerate(LOCAL):
            f[k] = edge(5 + i, t)
        for i, k in enumerate(IN):
            own = edge(OUT.index(OPP[k]), t)
            f[k] = stream_rim(lambda s, i=i: got[i, s], own, k, t, lane, row)
        g = collide(f, force_rim)
        for k in range(19):
            r2e[k, t] = g[k]
        f = [None] * 19
        for i, k in enumerate(LOCAL):
            f[FLIP[k]] = received(5 + i, t)
        for i, k in enumerate(OUT):
            own = got[IN.index(OPP[k]), t]
            f[k] = stream_rim(lambda s, i=i: edge(i, s), own, k, t, lane, row)
        g = collide(f, force_rim)
        for k in range(19):
            r2h[k, t] = g[k]
        for i in range(5):
            got2[i, t] = received(19 + i, t)

    def at(ref, index=None):
        return lambda k, s: ref[k if index is None else index.index(k), s]

    for t in range(9):
        for depth, (level, inward, outward) in enumerate(
            (
                (at(r2h), at(got2, IN), at(r2e)),
                (at(r2e), at(r2h), at(second)),
                (at(second), at(r2e), at(third, OUT)),
            )
        ):
            f = []
            for k in range(19):
                own = level(OPP[k], t)
                if k == 0:
                    f.append(own)
                    continue
                src = level if k in FLAT else (inward if k in IN else outward)
                f.append(stream_rim(lambda s, k=k, src=src: src(k, s), own, k, t, lane, row))
            g = collide(f, force_rim)
            for k in IN if depth == 0 else range(19):
                put(t, k, g[k], depth)

    writes = []
    for t in range(8):
        at = pl.ds(t * 128, 128)
        for p in range(4):
            f = stream_own(load3, p, t, lane)
            rho = f[0]
            for k in range(1, 19):
                rho = rho + f[k]
            solid = mask[p, :, at] > 0
            density[p, :, at] = jnp.where(solid, 0.0, rho)
            inv = (1.0 / MACH) / rho
            for a in range(3):
                plus = [f[k] for k in range(19) if VEL[k][a] == 1]
                minus = [f[k] for k in range(19) if VEL[k][a] == -1]
                j = plus[0] - minus[0]
                for x, y in zip(plus[1:], minus[1:]):
                    j = j + (x - y)
                velocity[a, p, :, at] = jnp.where(solid, 0.0, j * inv)
        if (t + 1) % WRITE == 0:
            done = pl.ds(128 * (t + 1 - WRITE), 128 * WRITE)
            writes.append(pltpu.make_async_copy(density.at[:, :, done], density_hbm.at[:, :, done], sem.at[len(writes)]))
            writes.append(
                pltpu.make_async_copy(velocity.at[:, :, :, done], velocity_hbm.at[:, :, :, done], sem.at[len(writes)])
            )
            for copy in writes[-2:]:
                copy.start()
    for copy in writes:
        copy.wait()


VMEM = pl.BlockSpec(memory_space=pltpu.VMEM)
HBM = pl.BlockSpec(memory_space=pltpu.HBM)


def call(kernel, name, us, out_shape, in_specs, out_specs, scratch, room=40):
    return pl.pallas_call(
        kernel,
        out_shape=out_shape,
        in_specs=in_specs,
        out_specs=out_specs,
        scratch_shapes=scratch,
        compiler_params=pltpu.CompilerParams(vmem_limit_bytes=room * 1024 * 1024),
        cost_estimate=pl.CostEstimate(
            flops=int(us * 1e6), bytes_accessed=int(us * 3e6), transcendentals=0
        ),
        name=name,
    )


def sds(*shape):
    return jax.ShapeDtypeStruct(shape, F32)


def buf(*shape):
    return pltpu.VMEM(shape, F32)


def swap(x, axis, parity):
    count = lax.axis_size(axis)
    pairs = [(i, (i + 1) % count if i % 2 == parity else (i - 1) % count) for i in range(count)]
    return lax.ppermute(x, axis, pairs)


def tiles(x):
    lead = x.shape[:-3]
    planes, height, width = x.shape[-3:]
    x = x.reshape(lead + (planes, height, width // 128, 128))
    x = jnp.swapaxes(x, -3, -2)
    return x.reshape(lead + (planes * height * width // 128, 128))


def local(pop, mask, force):
    far_memory = [pltpu.with_memory_space_constraint(x, pltpu.HBM) for x in (pop, mask, force)]
    z1, z0, mask, force = call(
        pack_kernel, "pack", 0.7,
        (sds(5, 8, 128), sds(5, 8, 128), jax.ShapeDtypeStruct(mask.shape, mask.dtype), sds(3, 8, 128)),
        [HBM] * 3, (VMEM,) * 4,
        [buf(19, 4, 8, 128), buf(19, 4, 8, 128), pltpu.SMEM((3,), F32),
         pltpu.SemaphoreType.DMA((2 + 2 * len(GROUPS),))],
    )(*far_memory)
    got1 = swap(z1, "gz", 1)
    got0 = swap(z0, "gz", 0)
    pop_tiles, mask_tiles = tiles(pop), tiles(mask)
    e1, e2, e3, inner, r1 = call(
        edge_kernel, "edge", 2.0,
        (sds(19, 64, 128), sds(19, 64, 128), sds(5, 64, 128), sds(6, NMSG, 8, 128),
         sds(OWN, 19, 32, 128)),
        [VMEM] * 3, (VMEM,) * 5, [],
    )(force, pop_tiles, mask_tiles)
    strip, outer, far, near = call(
        rim_kernel, "rim", 1.0,
        (sds(19, 32, 128), sds(3, 19, 8, 128), sds(194, 4, 128), sds(194, 4, 128)),
        [VMEM] * 7, (VMEM,) * 4,
        [buf(19, 8, 128), buf(19, 8, 128), buf(5, 8, 128)],
    )(force, e1, e2, e3, inner, got1, got0)
    far = swap(far, "gy", 1)
    near = swap(near, "gy", 0)
    r3, second, third = call(
        middle_kernel, "middle", 3.0,
        (sds(9, 19, 32, 128), sds(19, 9, 8, 128), sds(5, 9, 8, 128)), [VMEM] * 5, (VMEM,) * 3,
        [buf(8 - OWN, 19, 32, 128), buf(19, 32, 128), buf(9, 19, 32, 128)],
    )(force, pop_tiles, mask_tiles, r1, strip)
    return call(
        last_kernel, "last", 4.0,
        (sds(4, 8, 1024), sds(3, 4, 8, 1024)),
        [VMEM] * 9, (HBM, HBM),
        [buf(9, 19, 40, 128), buf(5, 9, 8, 128), buf(5, 9, 8, 128),
         buf(19, 9, 8, 128), buf(19, 9, 8, 128), buf(4, 8, 1024), buf(3, 4, 8, 1024),
         pltpu.SemaphoreType.DMA((16 // WRITE,))],
    )(force, r3, second, third, inner, outer, far, near, mask)


def solution(mesh):
    return jax.shard_map(
        local,
        mesh=mesh,
        in_specs=(P(None, None, "gy", "gz"), P(None, "gy", "gz"), P()),
        out_specs=(P(None, "gy", "gz"), P(None, None, "gy", "gz")),
        check_vma=False,
    )
```

```python
import jax
import jax.numpy as jnp
from jax import lax
from jax.experimental import pallas as pl
from jax.experimental.pallas import tpu as pltpu
from jax.sharding import PartitionSpec as P

VEL = [
    (0, 0, 0),
    (1, 0, 0),
    (-1, 0, 0),
    (0, 1, 0),
    (0, -1, 0),
    (0, 0, 1),
    (0, 0, -1),
    (1, 1, 0),
    (-1, -1, 0),
    (1, -1, 0),
    (-1, 1, 0),
    (1, 0, 1),
    (-1, 0, -1),
    (1, 0, -1),
    (-1, 0, 1),
    (0, 1, 1),
    (0, -1, -1),
    (0, 1, -1),
    (0, -1, 1),
]
OPP = [VEL.index((-x, -y, -z)) for x, y, z in VEL]
FLIP = [VEL.index((x, -y, z)) for x, y, z in VEL]
IN = [k for k in range(19) if VEL[k][1] == 1]
OUT = [FLIP[k] for k in IN]
FLAT = [k for k in range(19) if VEL[k][1] == 0]
LOCAL = FLAT + OUT
NMSG = 24
MACH = 0.05
BIG = 1e30
NAN = float("nan")
F32 = jnp.float32


def lanes():
    return lax.broadcasted_iota(jnp.int32, (8, 128), 1)


def rows():
    return lax.broadcasted_iota(jnp.int32, (8, 128), 0)


def collide(f, force):
    fx, fy, fz = force
    sx, dx = f[1] + f[2], f[1] - f[2]
    sy, dy = f[3] + f[4], f[3] - f[4]
    sz, dz = f[5] + f[6], f[5] - f[6]

    def plane(a):
        big, small = f[a] + f[a + 1], f[a] - f[a + 1]
        big2, small2 = f[a + 2] + f[a + 3], f[a + 2] - f[a + 3]
        return big + big2, big - big2, small + small2, small - small2, (small, small2)

    nxy, mxy, tyyx, txxy, odd_xy = plane(7)
    nxz, mxz, tzzx, txxz, odd_xz = plane(11)
    nyz, myz, tzzy, tyyz, odd_yz = plane(15)
    tx, ty, tz = tyyx + tzzx, txxy + tzzy, txxz + tyyz
    jx, jy, jz = dx + tx, dy + ty, dz + tz
    nx, ny, nz = nxy + nxz, nxy + nyz, nxz + nyz
    total_s = (sx + sy) + sz
    total_n = nx + nyz
    rho = (f[0] + total_s) + total_n
    inv = 0.3125 / rho
    vx, vy, vz = jx * inv, jy * inv, jz * inv
    gx, gy, gz = jx * vx, jy * vy, jz * vz
    total_g = (gx + gy) + gz
    mxy = jx * vy - 0.0625 * mxy
    mxz = jx * vz - 0.0625 * mxz
    myz = jy * vz - 0.0625 * myz
    base = rho * (1.3 / 36.0) + total_g * (1.3 / 3.75)
    nxy = (base - 0.52 * gz) - 0.075 * nxy
    nxz = (base - 0.52 * gy) - 0.075 * nxz
    nyz = (base - 0.52 * gx) - 0.075 * nyz
    bx = jx * (0.4 / 3.0) + fx * (1.0 / 12.0)
    by = jy * (0.4 / 3.0) + fy * (1.0 / 12.0)
    bz = jz * (0.4 / 3.0) + fz * (1.0 / 12.0)
    rest = rho * (1.25 / 6.0 - 5.2 / 36.0) + total_g * (1.04 - 5.2 / 3.75)
    out = [None] * 19

    def axis(a, g, s, n, d, t, force_a):
        even = ((rest + 0.96 * g) - 0.125 * s) + 0.025 * n
        odd = (0.8 / 3.0 * t - 0.1 / 3.0 * d) + force_a * (1.0 / 6.0)
        out[a], out[a + 1] = even + odd, even - odd

    def edge(a, n, m, b1, b2, p, q):
        big, big2 = n + m, n - m
        small, small2 = (b1 + b2) - 0.3 * p, (b1 - b2) - 0.3 * q
        out[a], out[a + 1] = big + small, big - small
        out[a + 2], out[a + 3] = big2 + small2, big2 - small2

    axis(1, gx, sx, nx, dx, tx, fx)
    axis(3, gy, sy, ny, dy, ty, fy)
    axis(5, gz, sz, nz, dz, tz, fz)
    edge(7, nxy, mxy, bx, by, *odd_xy)
    edge(11, nxz, mxz, bx, bz, *odd_xz)
    edge(15, nyz, myz, by, bz, *odd_yz)
    out[0] = (rho * (1.0 - 1.25 + 15.6 / 36.0) + total_g * (15.6 / 3.75 - 6.08)) + (
        0.25 * total_s + 0.2 * total_n
    )
    return out


def along_z(get, t, cz, lane):
    cur = get(t)
    if cz == 0:
        return cur
    if cz == 1:
        before = get((t + 8) % 9 if isinstance(t, int) else jnp.where(t == 0, 8, t - 1))
        return pltpu.roll(jnp.where(lane == 127, before, cur), 1, axis=1)
    after = get((t + 1) % 9 if isinstance(t, int) else jnp.where(t == 8, 0, t + 1))
    return pltpu.roll(jnp.where(lane == 0, after, cur), 127, axis=1)


def stream_own(load, p, t, lane):
    f = []
    for k in range(19):
        cx, cy, cz = VEL[k]
        own = load(OPP[k], t, p, 0)
        q = p - cx
        if k == 0 or q < 0 or q > 3:
            f.append(own)
            continue
        v = along_z(lambda s, k=k, q=q, cy=cy: load(k, s, q, cy), t, cz, lane)
        f.append(jnp.where(v < BIG, v, own))
    return f


def stream_rim(get, own, k, t, lane, row):
    cx, _, cz = VEL[k]
    v = along_z(get, t, cz, lane)
    if cx:
        v = pltpu.roll(v, cx % 8, axis=0)
        wall = (row & 3) == (0 if cx == 1 else 3)
        v = jnp.where(wall, NAN, v)
    return jnp.where(v < BIG, v, own)


def edges(ref, flipped, lower, upper):
    a = ref[pl.ds(lower, 4, stride=8), :]
    b = flipped[pl.ds(upper, 4, stride=8), :]
    return jnp.concatenate([a, b], axis=0)


def force_of(force_ref):
    return force_ref[0], force_ref[1], force_ref[2]


def rim_force(force, row):
    fx, fy, fz = force
    return fx, jnp.where(row < 4, fy, -fy), fz


GROUPS = ((0, 10), (10, 19))


def pack_kernel(pop_hbm, mask_hbm, force_hbm, out1, out0, mask, force, first, last, given, sem):
    copies = [
        pltpu.make_async_copy(mask_hbm, mask, sem.at[0]),
        pltpu.make_async_copy(force_hbm, given, sem.at[1]),
    ]
    for i, (a, b) in enumerate(GROUPS):
        for j, (at, to) in enumerate(((0, first), (896, last))):
            copies.append(
                pltpu.make_async_copy(
                    pop_hbm.at[a:b, :, :, at : at + 128], to.at[a:b], sem.at[2 + 2 * i + j]
                )
            )
    for copy in copies:
        copy.start()
    copies[0].wait()
    copies[1].wait()
    for i in range(3):
        force[i] = jnp.full((8, 128), given[i], F32)
    lane = lanes()
    even = lax.rem(lax.axis_index("gz"), 2) == 0
    group = lane // 8
    left = [jnp.zeros((8, 128), F32)] * 5
    right = [jnp.zeros((8, 128), F32)] * 5
    for n, (k0, k1) in enumerate(GROUPS):
        copies[2 + 2 * n].wait()
        copies[3 + 2 * n].wait()
        for k in range(k0, k1):
            for p in range(4):
                tile, s = divmod(4 * k + p, 16)
                a, b = first[k, p], last[k, p]
                if k == 0:
                    a = jnp.where(mask[p, :, 0:128] > 0, NAN, a)
                    b = jnp.where(mask[p, :, 896:1024] > 0, NAN, b)
                if s:
                    a = pltpu.roll(a, 8 * s, axis=1)
                    b = pltpu.roll(b, 8 * s, axis=1)
                left[tile] = jnp.where(group == s, a, left[tile])
                right[tile] = jnp.where(group == (s + 15) % 16, b, right[tile])
    for tile in range(5):
        out0[tile] = jnp.where(even, right[tile], left[tile])
        out1[tile] = jnp.where(even, left[tile], right[tile])


def rim_values(e1, e2, e3, t, force_rim, lane, row):
    own = [e1(k, t) for k in range(19)]
    values = [own[k] for k in OUT]
    for k in LOCAL:
        if k == 0:
            values.append(own[0])
        else:
            src = e1 if k in FLAT else e2
            values.append(stream_rim(lambda s, k=k, src=src: src(k, s), own[OPP[k]], k, t, lane, row))
    own = [e2(k, t) for k in range(19)]
    f = [own[0]]
    for k in range(1, 19):
        src = e2 if k in FLAT else (e1 if k in IN else e3)
        f.append(stream_rim(lambda s, k=k, src=src: src(k, s), own[OPP[k]], k, t, lane, row))
    g = collide(f, force_rim)
    return values + [g[k] for k in OUT]


OWN = 4


def relax_own(t, force, pop, mask, r1):
    for p in range(4):
        at = pl.ds(64 * p + 8 * t, 8)
        f = [pop[k, at, :] for k in range(19)]
        f[0] = jnp.where(mask[at, :] > 0, NAN, f[0])
        g = collide(f, force)
        for k in range(19):
            r1[t - (OWN if t >= OWN else 0), k, 8 * p : 8 * p + 8, :] = g[k]


def edge_kernel(force_ref, pop, mask, e1, e2, e3, inner, r1):
    lane, row = lanes(), rows()
    force = force_of(force_ref)
    force_rim = rim_force(force, row)
    mirrored = (force[0], -force[1], force[2])
    for depth, e in enumerate((e1, e2, e3)):
        for side in range(2):
            for p in range(4):
                at = pl.ds(64 * p + (7 - depth if side else depth), 8, stride=8)
                f = [pop[FLIP[k] if side else k, at, :] for k in range(19)]
                f[0] = jnp.where(mask[at, :] > 0, NAN, f[0])
                g = collide(f, mirrored if side else force)
                for i, k in enumerate(OUT if depth == 2 else range(19)):
                    e[i, pl.ds(4 * side + p, 8, stride=8), :] = g[k]

    def tile(e):
        return lambda k, t: e[OUT.index(k) if e is e3 else k, 8 * t : 8 * t + 8, :]

    for t in range(1, 7):
        values = rim_values(tile(e1), tile(e2), tile(e3), t, force_rim, lane, row)
        for i, v in enumerate(values):
            inner[t - 1, i] = v
    for t in range(OWN):
        relax_own(t, force, pop, mask, r1)


def rim_kernel(force_ref, e1, e2, e3, inner, got1, got0, strip, outer, far, near, h1, h2, h3):
    lane, row = lanes(), rows()
    force_rim = rim_force(force_of(force_ref), row)
    even_z = lax.rem(lax.axis_index("gz"), 2) == 0
    even_y = lax.rem(lax.axis_index("gy"), 2) == 0
    for tile in range(5):
        a, b = got0[tile], got1[tile]
        take_a = even_z == ((lane & 7) < 4)
        both = jnp.where(take_a, a, b)
        for s in range(16):
            i = tile * 16 + s
            if i >= 76:
                break
            k, p = i // 4, i % 4
            strip[k, 8 * p : 8 * p + 8, :] = pltpu.roll(both, 128 - 8 * s, axis=1) if s else both
    for depth, h in enumerate((h1, h2, h3)):
        f = [edges(strip.at[k], strip.at[FLIP[k]], depth, 7 - depth) for k in range(19)]
        g = collide(f, force_rim)
        for i, k in enumerate(OUT if depth == 2 else range(19)):
            h[i] = g[k]

    def halves(v):
        w = jnp.where(even_y, pltpu.roll(v, 4, axis=0), v)
        return w[4:8], w[0:4]

    packed = [jnp.zeros((8, 128), F32)] * 2
    for t in (8, 0, 7):
        values = rim_values(
            lambda k, s: h1[k] if s == 8 else e1[k, 8 * s : 8 * s + 8, :],
            lambda k, s: h2[k] if s == 8 else e2[k, 8 * s : 8 * s + 8, :],
            lambda k, s: h3[OUT.index(k)] if s == 8 else e3[OUT.index(k), 8 * s : 8 * s + 8, :],
            t, force_rim, lane, row,
        )
        for i, v in enumerate(values):
            if i < 19:
                outer[(0, 7, 8).index(t), i] = v
            if t == 8:
                tile, s = divmod(i, 16)
                packed[tile] = jnp.where(lane // 8 == s, pltpu.roll(v, (8 * s + 4) % 128, axis=1), packed[tile])
            else:
                far[8 * i + t], near[8 * i + t] = halves(v)
    for tile in range(2):
        far[192 + tile], near[192 + tile] = halves(packed[tile])
    for t in range(1, 7):
        for i in range(NMSG):
            far[8 * i + t], near[8 * i + t] = halves(inner[t - 1, i])


def middle_kernel(force_ref, pop, mask, r1, strip, r3, second, third, rest, last_tile, r2):
    lane = lanes()
    force = force_of(force_ref)

    for t in range(OWN, 8):
        relax_own(t, force, pop, mask, rest)
    for p in range(4):
        g = collide([strip[k, 8 * p : 8 * p + 8, :] for k in range(19)], force)
        for k in range(19):
            last_tile[k, 8 * p : 8 * p + 8, :] = g[k]

    def load1(k, s, p, cy):
        v = (last_tile if s == 8 else r1.at[s] if s < OWN else rest.at[s - OWN])[k, 8 * p : 8 * p + 8, :]
        return pltpu.roll(v, cy % 8, axis=0) if cy else v

    def load2(k, s, p, cy):
        v = r2[s, k, 8 * p : 8 * p + 8, :]
        return pltpu.roll(v, cy % 8, axis=0) if cy else v

    for load, after in ((load1, r2), (load2, r3)):
        for t in range(9):
            for p in range(4):
                g = collide(stream_own(load, p, t, lane), force)
                for k in range(19):
                    if t < 8 or after is r2 or VEL[k][2]:
                        after[t, k, 8 * p : 8 * p + 8, :] = g[k]

    for t in range(9):
        for k in range(19):
            second[k, t] = edges(r2.at[t, k], r2.at[t, FLIP[k]], 1, 6)
        for i, k in enumerate(OUT):
            third[i, t] = edges(r2.at[t, k], r2.at[t, FLIP[k]], 2, 5)


WRITE = 2


def last_kernel(
    force_ref, r3_in, second, third, inner, outer, far, near, mask, density_hbm, velocity_hbm,
    r3, got, got2, r2h, r2e, density, velocity, sem
):
    def load3(k, s, p, cy):
        return r3[s, k, pl.ds(10 * p + 1 - cy, 8), :]

    def put(t, k, v, depth):
        r3[t, k, pl.ds(depth, 4, stride=10), :] = v[0:4]
        r3[t, FLIP[k], pl.ds(9 - depth, 4, stride=10), :] = v[4:8]

    lane, row = lanes(), rows()
    force = force_of(force_ref)
    force_rim = rim_force(force, row)
    even_y = lax.rem(lax.axis_index("gy"), 2) == 0

    def halves(at):
        v = jnp.concatenate([near[at], far[at]], axis=0)
        return jnp.where(even_y, pltpu.roll(v, 4, axis=0), v)

    packed = [halves(192), halves(193)]

    def received(i, t):
        if t < 8:
            return halves(8 * i + t)
        tile, s = divmod(i, 16)
        return pltpu.roll(packed[tile], (124 - 8 * s) % 128, axis=1)

    def edge(i, t):
        return outer[(0, 7, 8).index(t), i] if t in (0, 7, 8) else inner[t - 1, i]

    for t in range(9):
        for i in range(5):
            got[i, t] = received(i, t)

    for t in range(9):
        for k in range(19):
            for p in range(4):
                if t < 8 or VEL[k][2]:
                    r3[t, k, pl.ds(10 * p + 1, 8), :] = r3_in[t, k, 8 * p : 8 * p + 8, :]
        f = [None] * 19
        for i, k in enumerate(LOCAL):
            f[k] = edge(5 + i, t)
        for i, k in enumerate(IN):
            own = edge(OUT.index(OPP[k]), t)
            f[k] = stream_rim(lambda s, i=i: got[i, s], own, k, t, lane, row)
        g = collide(f, force_rim)
        for k in range(19):
            r2e[k, t] = g[k]
        f = [None] * 19
        for i, k in enumerate(LOCAL):
            f[FLIP[k]] = received(5 + i, t)
        for i, k in enumerate(OUT):
            own = got[IN.index(OPP[k]), t]
            f[k] = stream_rim(lambda s, i=i: edge(i, s), own, k, t, lane, row)
        g = collide(f, force_rim)
        for k in range(19):
            r2h[k, t] = g[k]
        for i in range(5):
            got2[i, t] = received(19 + i, t)

    def at(ref, index=None):
        return lambda k, s: ref[k if index is None else index.index(k), s]

    for t in range(9):
        for depth, (level, inward, outward) in enumerate(
            (
                (at(r2h), at(got2, IN), at(r2e)),
                (at(r2e), at(r2h), at(second)),
                (at(second), at(r2e), at(third, OUT)),
            )
        ):
            f = []
            for k in range(19):
                own = level(OPP[k], t)
                if k == 0:
                    f.append(own)
                    continue
                src = level if k in FLAT else (inward if k in IN else outward)
                f.append(stream_rim(lambda s, k=k, src=src: src(k, s), own, k, t, lane, row))
            g = collide(f, force_rim)
            for k in IN if depth == 0 else range(19):
                if t < 8 or VEL[k][2]:
                    put(t, k, g[k], depth)

    writes = []
    for t in range(8):
        at = pl.ds(t * 128, 128)
        for p in range(4):
            f = stream_own(load3, p, t, lane)
            rho = f[0]
            for k in range(1, 19):
                rho = rho + f[k]
            solid = mask[p, :, at] > 0
            density[p, :, at] = jnp.where(solid, 0.0, rho)
            inv = (1.0 / MACH) / rho
            for a in range(3):
                plus = [f[k] for k in range(19) if VEL[k][a] == 1]
                minus = [f[k] for k in range(19) if VEL[k][a] == -1]
                j = plus[0] - minus[0]
                for x, y in zip(plus[1:], minus[1:]):
                    j = j + (x - y)
                velocity[a, p, :, at] = jnp.where(solid, 0.0, j * inv)
        if (t + 1) % WRITE == 0:
            done = pl.ds(128 * (t + 1 - WRITE), 128 * WRITE)
            writes.append(pltpu.make_async_copy(density.at[:, :, done], density_hbm.at[:, :, done], sem.at[len(writes)]))
            writes.append(
                pltpu.make_async_copy(velocity.at[:, :, :, done], velocity_hbm.at[:, :, :, done], sem.at[len(writes)])
            )
            for copy in writes[-2:]:
                copy.start()
    for copy in writes:
        copy.wait()


VMEM = pl.BlockSpec(memory_space=pltpu.VMEM)
HBM = pl.BlockSpec(memory_space=pltpu.HBM)


def call(kernel, name, us, out_shape, in_specs, out_specs, scratch, room=40):
    return pl.pallas_call(
        kernel,
        out_shape=out_shape,
        in_specs=in_specs,
        out_specs=out_specs,
        scratch_shapes=scratch,
        compiler_params=pltpu.CompilerParams(vmem_limit_bytes=room * 1024 * 1024),
        cost_estimate=pl.CostEstimate(
            flops=int(us * 1e6), bytes_accessed=int(us * 3e6), transcendentals=0
        ),
        name=name,
    )


def sds(*shape):
    return jax.ShapeDtypeStruct(shape, F32)


def buf(*shape):
    return pltpu.VMEM(shape, F32)


def swap(x, axis, parity):
    count = lax.axis_size(axis)
    pairs = [(i, (i + 1) % count if i % 2 == parity else (i - 1) % count) for i in range(count)]
    return lax.ppermute(x, axis, pairs)


def tiles(x):
    lead = x.shape[:-3]
    planes, height, width = x.shape[-3:]
    x = x.reshape(lead + (planes, height, width // 128, 128))
    x = jnp.swapaxes(x, -3, -2)
    return x.reshape(lead + (planes * height * width // 128, 128))


def local(pop, mask, force):
    far_memory = [pltpu.with_memory_space_constraint(x, pltpu.HBM) for x in (pop, mask, force)]
    z1, z0, mask, force = call(
        pack_kernel, "pack", 0.7,
        (sds(5, 8, 128), sds(5, 8, 128), jax.ShapeDtypeStruct(mask.shape, mask.dtype), sds(3, 8, 128)),
        [HBM] * 3, (VMEM,) * 4,
        [buf(19, 4, 8, 128), buf(19, 4, 8, 128), pltpu.SMEM((3,), F32),
         pltpu.SemaphoreType.DMA((2 + 2 * len(GROUPS),))],
    )(*far_memory)
    got1 = swap(z1, "gz", 1)
    got0 = swap(z0, "gz", 0)
    pop_tiles, mask_tiles = tiles(pop), tiles(mask)
    e1, e2, e3, inner, r1 = call(
        edge_kernel, "edge", 2.0,
        (sds(19, 64, 128), sds(19, 64, 128), sds(5, 64, 128), sds(6, NMSG, 8, 128),
         sds(OWN, 19, 32, 128)),
        [VMEM] * 3, (VMEM,) * 5, [],
    )(force, pop_tiles, mask_tiles)
    strip, outer, far, near = call(
        rim_kernel, "rim", 1.0,
        (sds(19, 32, 128), sds(3, 19, 8, 128), sds(194, 4, 128), sds(194, 4, 128)),
        [VMEM] * 7, (VMEM,) * 4,
        [buf(19, 8, 128), buf(19, 8, 128), buf(5, 8, 128)],
    )(force, e1, e2, e3, inner, got1, got0)
    far = swap(far, "gy", 1)
    near = swap(near, "gy", 0)
    r3, second, third = call(
        middle_kernel, "middle", 3.0,
        (sds(9, 19, 32, 128), sds(19, 9, 8, 128), sds(5, 9, 8, 128)), [VMEM] * 5, (VMEM,) * 3,
        [buf(8 - OWN, 19, 32, 128), buf(19, 32, 128), buf(9, 19, 32, 128)],
    )(force, pop_tiles, mask_tiles, r1, strip)
    return call(
        last_kernel, "last", 4.0,
        (sds(4, 8, 1024), sds(3, 4, 8, 1024)),
        [VMEM] * 9, (HBM, HBM),
        [buf(9, 19, 40, 128), buf(5, 9, 8, 128), buf(5, 9, 8, 128),
         buf(19, 9, 8, 128), buf(19, 9, 8, 128), buf(4, 8, 1024), buf(3, 4, 8, 1024),
         pltpu.SemaphoreType.DMA((16 // WRITE,))],
    )(force, r3, second, third, inner, outer, far, near, mask)


def solution(mesh):
    return jax.shard_map(
        local,
        mesh=mesh,
        in_specs=(P(None, None, "gy", "gz"), P(None, "gy", "gz"), P()),
        out_specs=(P(None, "gy", "gz"), P(None, None, "gy", "gz")),
        check_vma=False,
    )
```
